128 devices in a mesh: ctx: 32 (over z, x, core), tp: 4 (over y).
Axes of the slice: x: 4, y: 4, z: 4, core: 2. Of those that a mesh axis runs over, the one named last changes fastest.
Arguments:
- queries: bfloat16 [32768, 4096], P(('ctx', 'tp')), may hold values from -40 to 40
- keys_in: bfloat16 [32768, 1024], P(('ctx', 'tp')), may hold values from -4 to 4
- values_in: bfloat16 [32768, 1024], P(('ctx', 'tp')), may hold values from -6 to 6
- grad_output: bfloat16 [32768, 4096], P(('ctx', 'tp')), may hold values from -6 to 6
- beacon_keys: bfloat16 [4096, 1024], P('ctx', 'tp'), may hold values from -6 to 6
- beacon_values: bfloat16 [4096, 1024], P('ctx', 'tp'), may hold values from -6 to 6
- read_blocks: int32 [32, 4], P('ctx'), may hold values from 0 to 30, as said below
- read_counts: int32 [32], P('ctx'), may hold values from 0 to 4, as said below
Outputs:
- attn_out: bfloat16 [32768, 4096], P(('ctx', 'tp'))
- grad_queries: bfloat16 [32768, 4096], P(('ctx', 'tp'))
- grad_keys: bfloat16 [32768, 1024], P(('ctx', 'tp'))
- grad_values: bfloat16 [32768, 1024], P(('ctx', 'tp'))
- grad_beacon_keys: bfloat16 [4096, 1024], P('ctx', 'tp')
- grad_beacon_values: bfloat16 [4096, 1024], P('ctx', 'tp')
The draws below stay inside these ranges and needn't reach their ends.
Inputs may be any that keep to these rules, and one draw needn't show every extreme that they name: `read_blocks`: row s lists distinct blocks of earlier segments in its first read_counts[s] slots, block s - 1 first; unused slots hold 0. The last segment reads block 15 in its second slot. read_counts[s] is at most min(s, 4); segment 0 reads nothing and the last segment uses all 4 slots.
All inputs are finite; a program needn't handle non-finite values.
Results may differ from the reference program's by a relative error of at most 0.01.
Values may be sent and summed in bfloat16 or wider, within the bound.
No kernel may reach another device: no remote copies, remote signals or barrier semaphores. Data moves between devices by JAX's collectives and lax.ppermute only.
A program may use at most 128 MiB of HBM per device.

```python
import jax
import jax.numpy as jnp
from jax import lax

HQ = 32
KVH = 8
HD = 128
SEG = 1024
NREAD = 4
BEAC = 128
NSEG = 32
TOKENS = 32768


def query_key_pair(key):
    query_seed = jax.random.fold_in(key, 101)
    key_seed = jax.random.fold_in(key, 102)
    query_vals = jax.random.truncated_normal(query_seed, -4.0, 4.0, (TOKENS, HQ * HD), jnp.float32)
    key_vals = jax.random.truncated_normal(key_seed, -4.0, 4.0, (TOKENS, KVH * HD), jnp.float32)
    return (query_vals, key_vals)


def draw_queries(key, part):
    return query_key_pair(key)[0].astype(jnp.bfloat16)


def draw_keys_in(key, part):
    return query_key_pair(key)[1].astype(jnp.bfloat16)


def shuffle_one(subkey):
    return jax.random.permutation(subkey, NSEG).astype(jnp.int32)


def read_lists(key):
    base = jax.random.fold_in(key, 303)
    count_seed, order_seed = jax.random.split(base)
    segments = jnp.arange(NSEG, dtype=jnp.int32)
    ceiling = jnp.minimum(segments, NREAD)
    counts = jax.random.randint(count_seed, (NSEG,), 1, NREAD + 1).astype(jnp.int32)
    counts = jnp.minimum(counts, ceiling)
    counts = jnp.where(segments == NSEG - 1, NREAD, counts).astype(jnp.int32)
    shuffled = jax.vmap(shuffle_one)(jax.random.split(order_seed, NSEG))
    block_ids = segments[None, :]
    scores = jnp.where(block_ids < segments[:, None], shuffled + 2, NSEG + 2 + block_ids)
    forced = (segments[:, None] == NSEG - 1) & (block_ids == NSEG // 2 - 1)
    scores = jnp.where(forced, 1, scores)
    scores = jnp.where(block_ids == segments[:, None] - 1, 0, scores)
    ranking = jnp.argsort(scores, axis=1, stable=True).astype(jnp.int32)[:, :NREAD]
    slots = jnp.arange(NREAD, dtype=jnp.int32)[None, :]
    blocks = jnp.where(slots < counts[:, None], ranking, 0).astype(jnp.int32)
    return (blocks, counts)


def draw_read_blocks(key, part):
    return read_lists(key)[0]


def draw_read_counts(key, part):
    return read_lists(key)[1]


def shard_levels(key, shape, pieces, smallest, largest):
    def one(position, blocks):
        draws = jax.random.uniform(jax.random.fold_in(jax.random.fold_in(key, 6), position), (blocks,), jnp.float32, smallest / len(pieces), largest / len(pieces))
        return jnp.repeat(jnp.exp(draws), shape[position] // blocks).reshape((-1,) + (1,) * (len(shape) - position - 1))

    factor_of = one(*pieces[0])
    for cut in pieces[1:]:
        factor_of = factor_of * one(*cut)
    return factor_of


def gaussian(rng, shape, spread, limit, cuts=(), kind=jnp.bfloat16):
    gain = shard_levels(rng, shape, cuts, -0.22, 0.18) if cuts else 1.0
    drawn = jax.random.normal(rng, shape, jnp.float32) * spread * gain
    return jnp.minimum(jnp.maximum(drawn, -limit), limit).astype(kind)


def setup_inputs(seed: int = 0) -> dict:
    streams_of = jax.random.split(jax.random.key(seed), 9)
    queries = draw_queries(jax.random.fold_in(streams_of[8], 71), 0)
    keys_in = draw_keys_in(jax.random.fold_in(streams_of[8], 71), 0)
    values_in = gaussian(streams_of[2], (TOKENS, KVH * HD), 1.0, 6.0, ((0, 128),))
    grad_output = gaussian(streams_of[3], (TOKENS, HQ * HD), 1.0, 6.0, ((0, 128),))
    beacon_keys = gaussian(streams_of[4], (NSEG * BEAC, KVH * HD), 1.0, 6.0, ((0, 32), (1, 4)))
    beacon_values = gaussian(streams_of[5], (NSEG * BEAC, KVH * HD), 1.0, 6.0, ((0, 32), (1, 4)))
    read_blocks = draw_read_blocks(jax.random.fold_in(streams_of[8], 71), 0)
    read_counts = draw_read_counts(jax.random.fold_in(streams_of[8], 71), 0)
    return {"queries": queries, "keys_in": keys_in, "values_in": values_in, "grad_output": grad_output, "beacon_keys": beacon_keys, "beacon_values": beacon_values, "read_blocks": read_blocks, "read_counts": read_counts}


def head_grads(query_rows, key_rows, value_rows, grad_rows, allowed, score_scale):
    scores = jnp.dot(query_rows, key_rows.T, preferred_element_type=jnp.float32) * score_scale
    scores = jnp.where(allowed, scores, -1e30)
    row_max = jnp.max(scores, axis=1, keepdims=True)
    weights = jnp.exp(scores - row_max)
    prob_full = weights / jnp.sum(weights, axis=1, keepdims=True)
    prob_half = prob_full.astype(jnp.bfloat16)
    output = jnp.dot(prob_half, value_rows, preferred_element_type=jnp.float32).astype(jnp.bfloat16)
    grad_prob = jnp.dot(grad_rows, value_rows.T, preferred_element_type=jnp.float32)
    row_delta = jnp.sum(grad_rows.astype(jnp.float32) * output.astype(jnp.float32), axis=1, keepdims=True)
    dscores = (prob_full * (grad_prob - row_delta) * score_scale).astype(jnp.bfloat16)
    grad_query = jnp.dot(dscores, key_rows, preferred_element_type=jnp.float32).astype(jnp.bfloat16)
    grad_key = jnp.dot(dscores.T, query_rows, preferred_element_type=jnp.float32)
    grad_value = jnp.dot(prob_half.T, grad_rows, preferred_element_type=jnp.float32)
    return output, grad_query, grad_key, grad_value


def reference(queries, keys_in, values_in, grad_output, beacon_keys, beacon_values, read_blocks, read_counts):
    score_scale = HD ** -0.5
    group_size = HQ // KVH
    beacon_rows = NREAD * BEAC
    col_width = KVH * HD
    positions = jnp.arange(SEG, dtype=jnp.int32)
    causal = positions[None, :] <= positions[:, None]
    blocks_k = beacon_keys.reshape(NSEG, BEAC, col_width)
    blocks_v = beacon_values.reshape(NSEG, BEAC, col_width)

    def segment(totals, inputs):
        dense_k, dense_v = totals
        seg_q, seg_k, seg_v, seg_g, read_row, read_count = inputs
        slot_ok = jnp.arange(NREAD, dtype=jnp.int32) < read_count
        valid_keys = jnp.repeat(slot_ok, BEAC)
        allowed = jnp.concatenate([causal, jnp.broadcast_to(valid_keys[None, :], (SEG, beacon_rows))], axis=1)
        chosen_k = jnp.take(blocks_k, read_row, axis=0).reshape(beacon_rows, col_width)
        chosen_v = jnp.take(blocks_v, read_row, axis=0).reshape(beacon_rows, col_width)
        query_heads = seg_q.reshape(SEG, HQ, HD).transpose(1, 0, 2)
        grad_heads = seg_g.reshape(SEG, HQ, HD).transpose(1, 0, 2)
        key_heads = jnp.concatenate([seg_k, chosen_k], axis=0).reshape(SEG + beacon_rows, KVH, HD).transpose(1, 0, 2)
        value_heads = jnp.concatenate([seg_v, chosen_v], axis=0).reshape(SEG + beacon_rows, KVH, HD).transpose(1, 0, 2)

        def per_head(head_index):
            shared = head_index // group_size
            return head_grads(query_heads[head_index], key_heads[shared], value_heads[shared], grad_heads[head_index], allowed, score_scale)

        outputs, grad_query, grad_key, grad_value = lax.map(per_head, jnp.arange(HQ, dtype=jnp.int32))
        grad_key = jnp.sum(grad_key.reshape(KVH, group_size, SEG + beacon_rows, HD), axis=1)
        grad_value = jnp.sum(grad_value.reshape(KVH, group_size, SEG + beacon_rows, HD), axis=1)
        local_k = grad_key[:, :SEG].transpose(1, 0, 2).reshape(SEG, col_width).astype(jnp.bfloat16)
        local_v = grad_value[:, :SEG].transpose(1, 0, 2).reshape(SEG, col_width).astype(jnp.bfloat16)
        slot_mask = slot_ok.astype(jnp.float32)[:, None, None]
        part_k = grad_key[:, SEG:].transpose(1, 0, 2).reshape(NREAD, BEAC, col_width) * slot_mask
        part_v = grad_value[:, SEG:].transpose(1, 0, 2).reshape(NREAD, BEAC, col_width) * slot_mask
        dense_k = dense_k.at[read_row].add(part_k)
        dense_v = dense_v.at[read_row].add(part_v)
        seg_out = outputs.transpose(1, 0, 2).reshape(SEG, HQ * HD)
        seg_gq = grad_query.transpose(1, 0, 2).reshape(SEG, HQ * HD)
        return (dense_k, dense_v), (seg_out, seg_gq, local_k, local_v)

    start = (jnp.zeros((NSEG, BEAC, col_width), jnp.float32), jnp.zeros((NSEG, BEAC, col_width), jnp.float32))
    inputs = (queries.reshape(NSEG, SEG, HQ * HD), keys_in.reshape(NSEG, SEG, col_width),
              values_in.reshape(NSEG, SEG, col_width), grad_output.reshape(NSEG, SEG, HQ * HD),
              read_blocks, read_counts)
    (dense_k, dense_v), (all_out, all_gq, all_gk, all_gv) = lax.scan(segment, start, inputs)
    return (all_out.reshape(TOKENS, HQ * HD), all_gq.reshape(TOKENS, HQ * HD),
            all_gk.reshape(TOKENS, col_width), all_gv.reshape(TOKENS, col_width),
            dense_k.reshape(NSEG * BEAC, col_width).astype(jnp.bfloat16),
            dense_v.reshape(NSEG * BEAC, col_width).astype(jnp.bfloat16))
```

```python
import functools
import math

import jax
import jax.numpy as jnp
from jax import lax
from jax.experimental import pallas as pl
from jax.experimental.pallas import tpu as pltpu
from jax.sharding import Mesh
from jax.sharding import PartitionSpec as P

HD = 128
SCALE = HD**-0.5
SCALE2 = SCALE * math.log2(math.e)
NEG = -1e30
F32 = jnp.float32
BF16 = jnp.bfloat16
NN = (((1,), (0,)), ((), ()))
NT = (((1,), (1,)), ((), ()))
TN = (((0,), (0,)), ((), ()))
TP = 4
CHUNK = 256
SLOTS = 4
BLOCK = 128
BEAC = SLOTS * BLOCK
KEYS = BEAC + TP * CHUNK
GROUP = 4
QW = GROUP * HD
PIECE = 2 * QW + 2 * HD


def mm(a, b, dims):
    return lax.dot_general(a, b, dims, preferred_element_type=F32)


def fold(x, op):
    return op(x.reshape(x.shape[0] // 8, 8, x.shape[1]), axis=0)


def chunk_grads(chunk, q, go, keys, vals, bias, scores, dk_acc, dv_acc):
    blocks = BEAC // CHUNK + chunk + 1
    peak = None
    for b in range(blocks):
        rows = pl.ds(b * CHUNK, CHUNK)
        s = mm(keys[rows, :], q, NT)
        if b < BEAC // CHUNK:
            part = bias[rows, :]
            s = s + jnp.concatenate([part, part], axis=1)
        if b == blocks - 1:
            key_pos = lax.broadcasted_iota(jnp.int32, (CHUNK, CHUNK), 0)
            query_pos = lax.broadcasted_iota(jnp.int32, (CHUNK, CHUNK), 1)
            s = jnp.where(key_pos <= query_pos, s, NEG)
        scores[rows, :] = s
        top = fold(s, jnp.max)
        peak = top if peak is None else jnp.maximum(peak, top)
    shift = jnp.max(peak, axis=0, keepdims=True) * SCALE2
    total = jnp.zeros((8, CHUNK), F32)
    for b in range(blocks):
        rows = pl.ds(b * CHUNK, CHUNK)
        w = jnp.exp2(scores[rows, :] * SCALE2 - shift)
        total = total + fold(w, jnp.sum)
        scores[rows, :] = w
    inv = 1.0 / jnp.sum(total, axis=0, keepdims=True)
    out = jnp.zeros((CHUNK, HD), F32)
    for b in range(blocks):
        rows = pl.ds(b * CHUNK, CHUNK)
        p = scores[rows, :] * inv
        scores[rows, :] = p
        pb = p.astype(BF16)
        dv_acc[rows, :] += mm(pb, go, NN)
        out = out + mm(pb, vals[rows, :], TN)
    out = out.astype(BF16)
    prod = go.astype(F32) * out.astype(F32)
    delta = lax.dot_general(
        jnp.ones((8, HD), F32), prod, NT, precision=lax.Precision.HIGHEST, preferred_element_type=F32
    )[0:1, :]
    dq = jnp.zeros((CHUNK, HD), F32)
    for b in range(blocks):
        rows = pl.ds(b * CHUNK, CHUNK)
        dp = mm(vals[rows, :], go, NT)
        ds = (scores[rows, :] * (dp - delta)).astype(BF16)
        dk_acc[rows, :] += mm(ds, q, NN)
        dq = dq + mm(ds, keys[rows, :], TN)
    return out, (dq * SCALE).astype(BF16)


S_A, S_B, S_COUNT, S_Y, S_SAME = 0, 4, 8, 9, 10


def attn_body(sc, *refs):
    pieces = [refs[4 * d : 4 * d + 4] for d in range(TP)]
    refs = refs[4 * TP :]
    near, far = refs[: 2 * SLOTS], refs[2 * SLOTS : 4 * SLOTS]
    refs = refs[4 * SLOTS :]
    outs, beac_out = refs[:TP], refs[TP]
    qs, gs, os, dqs, keys, vals, bias, scores, dk_acc, dv_acc = refs[TP + 1 :]
    head = pl.program_id(0)
    me = sc[S_Y]

    @pl.when(head == 0)
    def _():
        same = sc[S_SAME]
        for t, dst in ((0, keys), (1, vals)):
            for j in range(SLOTS):
                a, b = near[t * SLOTS + j][0], far[t * SLOTS + j][0]
                dst[pl.ds(j * BLOCK, BLOCK), :] = jnp.where(same == 1, a, b)
            for d in range(TP):
                at = pl.multiple_of(BEAC + lax.rem(me + d, TP) * CHUNK, CHUNK)
                dst[pl.ds(at, CHUNK), :] = pieces[d][2 + t][...]
        for j in range(SLOTS):
            row = jnp.where(j < sc[S_COUNT], 0.0, NEG)
            bias[pl.ds(j * BLOCK, BLOCK), :] = jnp.full((BLOCK, HD), row, F32)
        dk_acc[...] = jnp.zeros_like(dk_acc)
        dv_acc[...] = jnp.zeros_like(dv_acc)

    for d in range(TP):
        at = lax.rem(me + d, TP)
        qs[at] = pieces[d][0][...]
        gs[at] = pieces[d][1][...]
    for i in range(TP):
        o, dq = chunk_grads(i, qs[i], gs[i], keys, vals, bias, scores, dk_acc, dv_acc)
        os[i] = o
        dqs[i] = dq
    at_o = pl.multiple_of(head * HD, HD)
    at_q = pl.multiple_of(QW + head * HD, HD)
    for d in range(TP):
        at = lax.rem(me + d, TP)
        outs[d][:, pl.ds(at_o, HD)] = os[at]
        outs[d][:, pl.ds(at_q, HD)] = dqs[at]

    @pl.when(head == GROUP - 1)
    def _():
        for d in range(TP):
            at = pl.multiple_of(BEAC + lax.rem(me + d, TP) * CHUNK, CHUNK)
            outs[d][:, 2 * QW : 2 * QW + HD] = (dk_acc[pl.ds(at, CHUNK), :] * SCALE).astype(BF16)
            outs[d][:, 2 * QW + HD :] = dv_acc[pl.ds(at, CHUNK), :].astype(BF16)
        for j in range(SLOTS):
            rows = pl.ds(j * BLOCK, BLOCK)
            beac_out[j, :, :HD] = (dk_acc[rows, :] * SCALE).astype(BF16)
            beac_out[j, :, HD:] = dv_acc[rows, :].astype(BF16)


def attn(group, scalars, own, pieces, near, far):
    spec = pl.BlockSpec
    ops, in_specs = [], []
    kv_heads = 2
    for t in range(2):
        ops.append(own[t])
        in_specs.append(
            spec((CHUNK, HD), lambda h, sc: (0, (sc[S_Y] * kv_heads + group) * GROUP + h))
        )
    for t in range(2):
        ops.append(own[2 + t])
        in_specs.append(spec((CHUNK, HD), lambda h, sc: (0, sc[S_Y] * kv_heads + group)))
    for piece in pieces:
        ops += [piece] * 4
        in_specs += [
            spec((CHUNK, HD), lambda h, sc: (0, h)),
            spec((CHUNK, HD), lambda h, sc: (0, GROUP + h)),
            spec((CHUNK, HD), lambda h, sc: (0, 2 * GROUP)),
            spec((CHUNK, HD), lambda h, sc: (0, 2 * GROUP + 1)),
        ]
    for arr, base in ((near, S_A), (far, S_B)):
        for t in range(2):
            for j in range(SLOTS):
                ops.append(arr)
                in_specs.append(
                    spec((1, BLOCK, HD), lambda h, sc, at=base + j, t=t: (sc[at], 0, t))
                )
    out_specs = [spec((CHUNK, PIECE), lambda h, sc: (0, 0)) for _ in range(TP)]
    out_specs.append(spec((SLOTS, BLOCK, 2 * HD), lambda h, sc: (0, 0, 0)))
    out_shape = [jax.ShapeDtypeStruct((CHUNK, PIECE), BF16) for _ in range(TP)]
    out_shape.append(jax.ShapeDtypeStruct((SLOTS, BLOCK, 2 * HD), BF16))
    pairs = GROUP * CHUNK * CHUNK * 18
    return pl.pallas_call(
        attn_body,
        grid_spec=pltpu.PrefetchScalarGridSpec(
            num_scalar_prefetch=1,
            grid=(GROUP,),
            in_specs=in_specs,
            out_specs=out_specs,
            scratch_shapes=[
                pltpu.VMEM((TP, CHUNK, HD), BF16),
                pltpu.VMEM((TP, CHUNK, HD), BF16),
                pltpu.VMEM((TP, CHUNK, HD), BF16),
                pltpu.VMEM((TP, CHUNK, HD), BF16),
                pltpu.VMEM((KEYS, HD), BF16),
                pltpu.VMEM((KEYS, HD), BF16),
                pltpu.VMEM((BEAC, HD), F32),
                pltpu.VMEM((KEYS, CHUNK), F32),
                pltpu.VMEM((KEYS, HD), F32),
                pltpu.VMEM((KEYS, HD), F32),
            ],
        ),
        out_shape=out_shape,
        compiler_params=pltpu.CompilerParams(vmem_limit_bytes=24 << 20),
        cost_estimate=pl.CostEstimate(
            flops=6 * 2 * pairs * HD * 2, bytes_accessed=6 << 20, transcendentals=pairs
        ),
        name="attn",
    )(scalars, *ops)


def place_body(y_ref, *refs):
    n = 2 * TP
    ins, outs, bufs, in_sems, out_sems = refs[:n], refs[n : n + 4], refs[n + 4], refs[n + 5], refs[n + 6]
    me = y_ref[0]
    loads = [pltpu.make_async_copy(ins[i], bufs.at[i], in_sems.at[i]) for i in range(n)]
    for copy in loads:
        copy.start()
    stores = []
    for i in range(n):
        group, d = divmod(i, TP)
        src = lax.rem(me + d, TP) * 2 + group
        loads[i].wait()
        for t, (at, width) in enumerate(((0, QW), (QW, QW), (2 * QW, HD), (2 * QW + HD, HD))):
            col = pl.multiple_of(src * width, HD)
            copy = pltpu.make_async_copy(
                bufs.at[i, :, pl.ds(at, width)], outs[t].at[:, pl.ds(col, width)], out_sems.at[i, t]
            )
            copy.start()
            stores.append(copy)
    for copy in stores:
        copy.wait()


def place(y, pieces):
    anyspec = pl.BlockSpec(memory_space=pl.ANY)
    widths = (TP * 2 * QW, TP * 2 * QW, TP * 2 * HD, TP * 2 * HD)
    return pl.pallas_call(
        place_body,
        grid_spec=pltpu.PrefetchScalarGridSpec(
            num_scalar_prefetch=1,
            grid=(),
            in_specs=[anyspec] * len(pieces),
            out_specs=[anyspec] * 4,
            scratch_shapes=[
                pltpu.VMEM((2 * TP, CHUNK, PIECE), BF16),
                pltpu.SemaphoreType.DMA((2 * TP,)),
                pltpu.SemaphoreType.DMA((2 * TP, 4)),
            ],
        ),
        out_shape=[jax.ShapeDtypeStruct((CHUNK, w), BF16) for w in widths],
        compiler_params=pltpu.CompilerParams(vmem_limit_bytes=16 << 20),
        name="place",
    )(y, *pieces)


def shift(x, step):
    return lax.ppermute(x, "y", [(s, (s + step) % TP) for s in range(TP)])


def swap(x):
    return lax.ppermute(x, "core", [(0, 1), (1, 0)])


def shards(queries, keys_in, values_in, grad_output, beacon_keys, beacon_values, read_blocks, read_counts):
    y = lax.axis_index("y")
    core = lax.axis_index("core")
    chips = lax.axis_size("z") * lax.axis_size("x")

    def cut(a, to, group, width):
        return lax.dynamic_slice(a, (0, (to * 2 + group) * width), (CHUNK, width))

    both = [
        jnp.concatenate(
            [beacon_keys[:, g * HD : (g + 1) * HD], beacon_values[:, g * HD : (g + 1) * HD]], axis=1
        )
        for g in range(2)
    ]
    first = core == 0
    mine = jnp.where(first, both[0], both[1])
    other = swap(jnp.where(first, both[1], both[0]))
    chip_blocks = jnp.broadcast_to(jnp.stack([mine, other])[None], (chips, 2, BLOCK, 2 * HD))
    row, count = read_blocks[0], read_counts
    table = jnp.concatenate([row, count])
    peer_table = swap(table)

    recv = []
    for g in range(2):
        got = {}
        for d in (1, 3, 2):
            to = (y + d) % TP
            piece = jnp.concatenate(
                [
                    cut(queries, to, g, QW),
                    cut(grad_output, to, g, QW),
                    cut(keys_in, to, g, HD),
                    cut(values_in, to, g, HD),
                ],
                axis=1,
            )
            got[TP - d] = shift(piece, d)
        recv.append([got[1], got[2], got[3]])

    near = lax.all_to_all(chip_blocks, ("z", "x"), 0, 0, tiled=True)
    far = swap(near).reshape(chips * 2, BLOCK, 2 * HD)
    near = near.reshape(chips * 2, BLOCK, 2 * HD)

    own = (queries, grad_output, keys_in, values_in)
    chip, parity = row // 2, row % 2
    tables = [table, peer_table]
    back, beacs = [], []
    for g in range(2):
        scalars = jnp.concatenate(
            [
                chip * 2 + (parity ^ core),
                chip * 2 + (parity ^ core ^ 1),
                count,
                y[None],
                (core == g).astype(jnp.int32)[None],
            ]
        ).astype(jnp.int32)
        res = attn(g, scalars, own, recv[g], near, far)
        got = {0: res[0]}
        for d in (1, 3, 2):
            got[TP - d] = shift(res[d], d)
        back.append([got[d] for d in range(TP)])
        dense = jnp.zeros((chips, BLOCK, 2 * HD), F32)
        ids = jnp.arange(chips, dtype=jnp.int32)
        for terms, tab in ((res[TP], table), (swap(res[TP]), peer_table)):
            for j in range(SLOTS):
                use = (tab[j] == ids * 2 + core) & (j < tab[SLOTS])
                dense = dense + jnp.where(use[:, None, None], terms[j].astype(F32)[None], 0.0)
        parts = lax.all_to_all(dense.astype(BF16), ("z", "x"), 0, 0, tiled=True)
        beacs.append(jnp.sum(parts.astype(F32), axis=0).astype(BF16))
    out, dq, dk, dv = place(y[None].astype(jnp.int32), back[0] + back[1])
    dbk = jnp.concatenate([b[:, :HD] for b in beacs], axis=1)
    dbv = jnp.concatenate([b[:, HD:] for b in beacs], axis=1)
    return out, dq, dk, dv, dbk, dbv


def solution(mesh):
    split = Mesh(mesh.devices.reshape(4, 4, 2, 4), ("z", "x", "core", "y"))
    ctx = ("z", "x", "core")
    tokens = P(ctx + ("y",), None)
    beacon = P(ctx, "y")
    in_specs = (tokens,) * 4 + (beacon,) * 2 + (P(ctx, None), P(ctx))
    out_specs = (tokens,) * 4 + (beacon,) * 2
    return jax.shard_map(shards, mesh=split, in_specs=in_specs, out_specs=out_specs, check_vma=False)
```

```python
import functools
import math

import jax
import jax.numpy as jnp
from jax import lax
from jax.experimental import pallas as pl
from jax.experimental.pallas import tpu as pltpu
from jax.sharding import Mesh
from jax.sharding import PartitionSpec as P


HD = 128
SCALE = HD**-0.5
SCALE2 = SCALE * math.log2(math.e)
NEG = -1e30
F32 = jnp.float32
BF16 = jnp.bfloat16
NN = (((1,), (0,)), ((), ()))
NT = (((1,), (1,)), ((), ()))
TN = (((0,), (0,)), ((), ()))
TP = 4
CHUNK = 256
SLOTS = 4
BLOCK = 128
BEAC = SLOTS * BLOCK
KEYS = BEAC + TP * CHUNK
GROUP = 4
QW = GROUP * HD
PIECE = 2 * QW + 2 * HD
SPANS = ((0, QW), (QW, QW), (2 * QW, HD), (2 * QW + HD, HD))


def mm(a, b, dims):
    return lax.dot_general(a, b, dims, preferred_element_type=F32)


def fold(x, op):
    return op(x.reshape(x.shape[0] // 8, 8, x.shape[1]), axis=0)


def chunk_grads(chunk, q, go, keys, vals, bias, scores, dk_acc, dv_acc):
    blocks = BEAC // CHUNK + chunk + 1
    peak = None
    for b in range(blocks):
        rows = pl.ds(b * CHUNK, CHUNK)
        s = mm(keys[rows, :], q, NT)
        if b < BEAC // CHUNK:
            part = bias[rows, :]
            s = s + jnp.concatenate([part, part], axis=1)
        if b == blocks - 1:
            key_pos = lax.broadcasted_iota(jnp.int32, (CHUNK, CHUNK), 0)
            query_pos = lax.broadcasted_iota(jnp.int32, (CHUNK, CHUNK), 1)
            s = jnp.where(key_pos <= query_pos, s, NEG)
        scores[rows, :] = s
        top = fold(s, jnp.max)
        peak = top if peak is None else jnp.maximum(peak, top)
    shift = jnp.max(peak, axis=0, keepdims=True) * SCALE2
    total = jnp.zeros((8, CHUNK), F32)
    for b in range(blocks):
        rows = pl.ds(b * CHUNK, CHUNK)
        w = jnp.exp2(scores[rows, :] * SCALE2 - shift)
        total = total + fold(w, jnp.sum)
        scores[rows, :] = w
    inv = 1.0 / jnp.sum(total, axis=0, keepdims=True)
    out = jnp.zeros((CHUNK, HD), F32)
    for b in range(blocks):
        rows = pl.ds(b * CHUNK, CHUNK)
        p = scores[rows, :] * inv
        scores[rows, :] = p
        pb = p.astype(BF16)
        dv_acc[rows, :] += mm(pb, go, NN)
        out = out + mm(pb, vals[rows, :], TN)
    out = out.astype(BF16)
    prod = go.astype(F32) * out.astype(F32)
    delta = lax.dot_general(
        jnp.ones((8, HD), F32), prod, NT, precision=lax.Precision.HIGHEST, preferred_element_type=F32
    )[0:1, :]
    dq = jnp.zeros((CHUNK, HD), F32)
    for b in range(blocks):
        rows = pl.ds(b * CHUNK, CHUNK)
        dp = mm(vals[rows, :], go, NT)
        ds = (scores[rows, :] * (dp - delta)).astype(BF16)
        dk_acc[rows, :] += mm(ds, q, NN)
        dq = dq + mm(ds, keys[rows, :], TN)
    return out, (dq * SCALE).astype(BF16)


S_A, S_B, S_COUNT, S_Y, S_SAME = 0, 4, 8, 9, 10


def attn_body(sc, *refs):
    pieces = [refs[4 * d : 4 * d + 4] for d in range(TP)]
    refs = refs[4 * TP :]
    near, far = refs[: 2 * SLOTS], refs[2 * SLOTS : 4 * SLOTS]
    refs = refs[4 * SLOTS :]
    outs, beac_out = refs[:TP], refs[TP]
    qs, gs, os, dqs, keys, vals, bias, scores, dk_acc, dv_acc = refs[TP + 1 :]
    head = pl.program_id(0)
    me = sc[S_Y]

    @pl.when(head == 0)
    def _():
        same = sc[S_SAME]
        for t, dst in ((0, keys), (1, vals)):
            for j in range(SLOTS):
                a, b = near[t * SLOTS + j][0], far[t * SLOTS + j][0]
                dst[pl.ds(j * BLOCK, BLOCK), :] = jnp.where(same == 1, a, b)
            for d in range(TP):
                at = pl.multiple_of(BEAC + lax.rem(me + d, TP) * CHUNK, CHUNK)
                dst[pl.ds(at, CHUNK), :] = pieces[d][2 + t][...]
        for j in range(SLOTS):
            row = jnp.where(j < sc[S_COUNT], 0.0, NEG)
            bias[pl.ds(j * BLOCK, BLOCK), :] = jnp.full((BLOCK, HD), row, F32)
        dk_acc[...] = jnp.zeros_like(dk_acc)
        dv_acc[...] = jnp.zeros_like(dv_acc)

    for d in range(TP):
        at = lax.rem(me + d, TP)
        qs[at] = pieces[d][0][...]
        gs[at] = pieces[d][1][...]
    for i in range(TP):
        o, dq = chunk_grads(i, qs[i], gs[i], keys, vals, bias, scores, dk_acc, dv_acc)
        os[i] = o
        dqs[i] = dq
    at_o = pl.multiple_of(head * HD, HD)
    at_q = pl.multiple_of(QW + head * HD, HD)
    for d in range(TP):
        at = lax.rem(me + d, TP)
        outs[d][:, pl.ds(at_o, HD)] = os[at]
        outs[d][:, pl.ds(at_q, HD)] = dqs[at]

    @pl.when(head == GROUP - 1)
    def _():
        for d in range(TP):
            at = pl.multiple_of(BEAC + lax.rem(me + d, TP) * CHUNK, CHUNK)
            outs[d][:, 2 * QW : 2 * QW + HD] = (dk_acc[pl.ds(at, CHUNK), :] * SCALE).astype(BF16)
            outs[d][:, 2 * QW + HD :] = dv_acc[pl.ds(at, CHUNK), :].astype(BF16)
        for j in range(SLOTS):
            rows = pl.ds(j * BLOCK, BLOCK)
            beac_out[j, :, :HD] = (dk_acc[rows, :] * SCALE).astype(BF16)
            beac_out[j, :, HD:] = dv_acc[rows, :].astype(BF16)


def attn(group, scalars, own, pieces, near, far):
    spec = pl.BlockSpec
    ops, in_specs = [], []
    kv_heads = 2
    for t in range(2):
        ops.append(own[t])
        in_specs.append(
            spec((CHUNK, HD), lambda h, sc: (0, (sc[S_Y] * kv_heads + group) * GROUP + h))
        )
    for t in range(2):
        ops.append(own[2 + t])
        in_specs.append(spec((CHUNK, HD), lambda h, sc: (0, sc[S_Y] * kv_heads + group)))
    for piece in pieces:
        ops += [piece] * 4
        in_specs += [
            spec((CHUNK, HD), lambda h, sc: (0, h)),
            spec((CHUNK, HD), lambda h, sc: (0, GROUP + h)),
            spec((CHUNK, HD), lambda h, sc: (0, 2 * GROUP)),
            spec((CHUNK, HD), lambda h, sc: (0, 2 * GROUP + 1)),
        ]
    for arr, base in ((near, S_A), (far, S_B)):
        for t in range(2):
            for j in range(SLOTS):
                ops.append(arr)
                in_specs.append(
                    spec((1, BLOCK, HD), lambda h, sc, at=base + j, t=t: (sc[at], 0, t))
                )
    out_specs = [spec((CHUNK, PIECE), lambda h, sc: (0, 0)) for _ in range(TP)]
    out_specs.append(spec((SLOTS, BLOCK, 2 * HD), lambda h, sc: (0, 0, 0)))
    out_shape = [jax.ShapeDtypeStruct((CHUNK, PIECE), BF16) for _ in range(TP)]
    out_shape.append(jax.ShapeDtypeStruct((SLOTS, BLOCK, 2 * HD), BF16))
    pairs = GROUP * CHUNK * CHUNK * 18
    return pl.pallas_call(
        attn_body,
        grid_spec=pltpu.PrefetchScalarGridSpec(
            num_scalar_prefetch=1,
            grid=(GROUP,),
            in_specs=in_specs,
            out_specs=out_specs,
            scratch_shapes=[
                pltpu.VMEM((TP, CHUNK, HD), BF16),
                pltpu.VMEM((TP, CHUNK, HD), BF16),
                pltpu.VMEM((TP, CHUNK, HD), BF16),
                pltpu.VMEM((TP, CHUNK, HD), BF16),
                pltpu.VMEM((KEYS, HD), BF16),
                pltpu.VMEM((KEYS, HD), BF16),
                pltpu.VMEM((BEAC, HD), F32),
                pltpu.VMEM((KEYS, CHUNK), F32),
                pltpu.VMEM((KEYS, HD), F32),
                pltpu.VMEM((KEYS, HD), F32),
            ],
        ),
        out_shape=out_shape,
        compiler_params=pltpu.CompilerParams(vmem_limit_bytes=60 << 20),
        cost_estimate=pl.CostEstimate(
            flops=6 * 2 * pairs * HD * 2, bytes_accessed=6 << 20, transcendentals=pairs
        ),
        name="attn",
    )(scalars, *ops)


def split_body(group, y_ref, *refs):
    ins, outs, bufs, in_sems, out_sems = refs[:4], refs[4:7], refs[7], refs[8], refs[9]
    me = y_ref[0]
    loads = []
    for i in range(TP - 1):
        src = lax.rem(me + i + 1, TP) * 2 + group
        row = []
        for t, (at, width) in enumerate(SPANS):
            col = pl.multiple_of(src * width, HD)
            copy = pltpu.make_async_copy(
                ins[t].at[:, pl.ds(col, width)], bufs.at[i, :, pl.ds(at, width)], in_sems.at[i, t]
            )
            copy.start()
            row.append(copy)
        loads.append(row)
    stores = []
    for i in range(TP - 1):
        for copy in loads[i]:
            copy.wait()
        copy = pltpu.make_async_copy(bufs.at[i], outs[i], out_sems.at[i])
        copy.start()
        stores.append(copy)
    for copy in stores:
        copy.wait()


def split(group, y, own):
    anyspec = pl.BlockSpec(memory_space=pl.ANY)
    return pl.pallas_call(
        functools.partial(split_body, group),
        grid_spec=pltpu.PrefetchScalarGridSpec(
            num_scalar_prefetch=1,
            grid=(),
            in_specs=[anyspec] * 4,
            out_specs=[anyspec] * (TP - 1),
            scratch_shapes=[
                pltpu.VMEM((TP - 1, CHUNK, PIECE), BF16),
                pltpu.SemaphoreType.DMA((TP - 1, 4)),
                pltpu.SemaphoreType.DMA((TP - 1,)),
            ],
        ),
        out_shape=[jax.ShapeDtypeStruct((CHUNK, PIECE), BF16)] * (TP - 1),
        compiler_params=pltpu.CompilerParams(vmem_limit_bytes=60 << 20),
        cost_estimate=pl.CostEstimate(flops=0, bytes_accessed=4 << 20, transcendentals=0),
        name="split",
    )(y, *own)


def place_body(y_ref, *refs):
    n = 2 * TP
    ins, outs, bufs, in_sems, out_sems = refs[:n], refs[n : n + 4], refs[n + 4], refs[n + 5], refs[n + 6]
    me = y_ref[0]
    loads = [pltpu.make_async_copy(ins[i], bufs.at[i], in_sems.at[i]) for i in range(n)]
    for copy in loads:
        copy.start()
    stores = []
    for i in range(n):
        group, d = divmod(i, TP)
        src = lax.rem(me + d, TP) * 2 + group
        loads[i].wait()
        for t, (at, width) in enumerate(SPANS):
            col = pl.multiple_of(src * width, HD)
            copy = pltpu.make_async_copy(
                bufs.at[i, :, pl.ds(at, width)], outs[t].at[:, pl.ds(col, width)], out_sems.at[i, t]
            )
            copy.start()
            stores.append(copy)
    for copy in stores:
        copy.wait()


def place(y, pieces):
    anyspec = pl.BlockSpec(memory_space=pl.ANY)
    widths = (TP * 2 * QW, TP * 2 * QW, TP * 2 * HD, TP * 2 * HD)
    return pl.pallas_call(
        place_body,
        grid_spec=pltpu.PrefetchScalarGridSpec(
            num_scalar_prefetch=1,
            grid=(),
            in_specs=[anyspec] * len(pieces),
            out_specs=[anyspec] * 4,
            scratch_shapes=[
                pltpu.VMEM((2 * TP, CHUNK, PIECE), BF16),
                pltpu.SemaphoreType.DMA((2 * TP,)),
                pltpu.SemaphoreType.DMA((2 * TP, 4)),
            ],
        ),
        out_shape=[jax.ShapeDtypeStruct((CHUNK, w), BF16) for w in widths],
        compiler_params=pltpu.CompilerParams(vmem_limit_bytes=60 << 20),
        name="place",
    )(y, *pieces)


def shift(x, step):
    return lax.ppermute(x, "y", [(s, (s + step) % TP) for s in range(TP)])


def to_chips(x):
    return lax.all_to_all(x, ("z", "x"), 0, 0, tiled=True)


def swap(x):
    return lax.ppermute(x, "core", [(0, 1), (1, 0)])


def layer(queries, keys_in, values_in, grad_output, beacon_keys, beacon_values, read_blocks, read_counts):
    y = lax.axis_index("y")
    core = lax.axis_index("core")
    chips = lax.axis_size("z") * lax.axis_size("x")

    both = [
        jnp.concatenate(
            [beacon_keys[:, g * HD : (g + 1) * HD], beacon_values[:, g * HD : (g + 1) * HD]], axis=1
        )
        for g in range(2)
    ]
    first = core == 0
    mine = jnp.where(first, both[0], both[1])
    other = swap(jnp.where(first, both[1], both[0]))
    chip_blocks = jnp.broadcast_to(jnp.stack([mine, other])[None], (chips, 2, BLOCK, 2 * HD))
    row, count = read_blocks[0], read_counts
    table = jnp.concatenate([row, count])
    peer_table = swap(table)

    own = (queries, grad_output, keys_in, values_in)
    place_at = y[None].astype(jnp.int32)
    recv = []
    for g in range(2):
        got = {}
        sent = split(g, place_at, own)
        for d in (1, 3, 2):
            got[TP - d] = shift(sent[d - 1], d)
        recv.append([got[1], got[2], got[3]])

    near = to_chips(chip_blocks)
    far = swap(near).reshape(chips * 2, BLOCK, 2 * HD)
    near = near.reshape(chips * 2, BLOCK, 2 * HD)

    chip, parity = row // 2, row % 2
    back, beacs = [], []
    for g in range(2):
        scalars = jnp.concatenate(
            [
                chip * 2 + (parity ^ core),
                chip * 2 + (parity ^ core ^ 1),
                count,
                y[None],
                (core == g).astype(jnp.int32)[None],
            ]
        ).astype(jnp.int32)
        res = attn(g, scalars, own, recv[g], near, far)
        got = {0: res[0]}
        for d in (1, 3, 2):
            got[TP - d] = shift(res[d], d)
        back.append([got[d] for d in range(TP)])
        dense = jnp.zeros((chips, BLOCK, 2 * HD), F32)
        ids = jnp.arange(chips, dtype=jnp.int32)
        for terms, tab in ((res[TP], table), (swap(res[TP]), peer_table)):
            for j in range(SLOTS):
                use = (tab[j] == ids * 2 + core) & (j < tab[SLOTS])
                dense = dense + jnp.where(use[:, None, None], terms[j].astype(F32)[None], 0.0)
        parts = to_chips(dense.astype(BF16))
        beacs.append(jnp.sum(parts.astype(F32), axis=0).astype(BF16))
    out, dq, dk, dv = place(place_at, back[0] + back[1])
    dbk = jnp.concatenate([b[:, :HD] for b in beacs], axis=1)
    dbv = jnp.concatenate([b[:, HD:] for b in beacs], axis=1)
    return out, dq, dk, dv, dbk, dbv


def solution(mesh):
    split = Mesh(mesh.devices.reshape(4, 4, 2, 4), ("z", "x", "core", "y"))
    ctx = ("z", "x", "core")
    tokens = P(ctx + ("y",), None)
    beacon = P(ctx, "y")
    in_specs = (tokens,) * 4 + (beacon,) * 2 + (P(ctx, None), P(ctx))
    out_specs = (tokens,) * 4 + (beacon,) * 2
    return jax.shard_map(layer, mesh=split, in_specs=in_specs, out_specs=out_specs, check_vma=False)
```

```python
import functools
import math

import jax
import jax.numpy as jnp
from jax import lax
from jax.experimental import pallas as pl
from jax.experimental.pallas import tpu as pltpu
from jax.sharding import Mesh
from jax.sharding import PartitionSpec as P


HD = 128
SCALE = HD**-0.5
SCALE2 = SCALE * math.log2(math.e)
NEG = -1e30
F32 = jnp.float32
BF16 = jnp.bfloat16
NN = (((1,), (0,)), ((), ()))
NT = (((1,), (1,)), ((), ()))
TP = 4
CHUNK = 256
SLOTS = 4
BLOCK = 128
BEAC = SLOTS * BLOCK
KEYS = BEAC + TP * CHUNK
GROUP = 4
QW = GROUP * HD
PIECE = 2 * QW + 2 * HD
SPANS = ((0, QW), (QW, QW), (2 * QW, HD), (2 * QW + HD, HD))


def mm(a, b, dims):
    return lax.dot_general(a, b, dims, preferred_element_type=F32)


def fold(x, op):
    return op(x.reshape(x.shape[0] // 8, 8, x.shape[1]), axis=0)


def chunk_steps(chunk, q_ref, go_ref, o_ref, dq_ref, keys, vals, keys_t, vals_t, bias, scores, probs, dscores):
    blocks = BEAC // CHUNK + chunk + 1
    depth = blocks * CHUNK
    cols = slice(chunk * CHUNK, (chunk + 1) * CHUNK)
    scores = scores.at[chunk]
    held = {}

    def at(b):
        return pl.ds(b * CHUNK, CHUNK)

    def score(b):
        s = mm(keys[at(b), :], q_ref[chunk], NT)
        if b < BEAC // CHUNK:
            part = bias[at(b), :]
            s = s + jnp.concatenate([part, part], axis=1)
        if b == blocks - 1:
            key_pos = lax.broadcasted_iota(jnp.int32, (CHUNK, CHUNK), 0)
            query_pos = lax.broadcasted_iota(jnp.int32, (CHUNK, CHUNK), 1)
            s = jnp.where(key_pos <= query_pos, s, NEG)
        scores[at(b), :] = s
        top = fold(s, jnp.max)
        held["top"] = top if b == 0 else jnp.maximum(held["top"], top)

    def peak():
        held["shift"] = jnp.max(held["top"], axis=0, keepdims=True) * SCALE2
        held["sum"] = jnp.zeros((8, CHUNK), F32)

    def weigh(b):
        w = jnp.exp2(scores[at(b), :] * SCALE2 - held["shift"])
        held["sum"] = held["sum"] + fold(w, jnp.sum)
        scores[at(b), :] = w

    def invert():
        held["inv"] = 1.0 / jnp.sum(held["sum"], axis=0, keepdims=True)

    def normal(b):
        p = scores[at(b), :] * held["inv"]
        scores[at(b), :] = p
        probs[at(b), cols] = p.astype(BF16)

    def attend():
        out = mm(vals_t[:, :depth], probs[:depth, cols], NN).T.astype(BF16)
        o_ref[chunk] = out
        prod = go_ref[chunk].astype(F32) * out.astype(F32)
        held["delta"] = lax.dot_general(
            jnp.ones((8, HD), F32), prod, NT, precision=lax.Precision.HIGHEST, preferred_element_type=F32
        )[0:1, :]

    def dscore(b):
        dp = mm(vals[at(b), :], go_ref[chunk], NT)
        dscores[at(b), cols] = (scores[at(b), :] * (dp - held["delta"])).astype(BF16)

    def dquery():
        dq_ref[chunk] = (mm(keys_t[:, :depth], dscores[:depth, cols], NN).T * SCALE).astype(BF16)

    each = range(blocks)
    steps = [functools.partial(score, b) for b in each] + [peak]
    steps += [functools.partial(weigh, b) for b in each] + [invert]
    steps += [functools.partial(normal, b) for b in each] + [attend]
    return steps + [functools.partial(dscore, b) for b in each] + [dquery]


def interleave(sequences, lag):
    items, start = [], 0.0
    for n, steps in enumerate(sequences):
        items += [(start + t, n, step) for t, step in enumerate(steps)]
        start += lag * len(steps)
    for _, _, step in sorted(items, key=lambda item: item[:2]):
        step()


S_A, S_B, S_COUNT, S_Y, S_SAME = 0, 4, 8, 9, 10


def attn_body(sc, *refs):
    pieces = [refs[4 * d : 4 * d + 4] for d in range(TP)]
    refs = refs[4 * TP :]
    near, far = refs[: 2 * SLOTS], refs[2 * SLOTS : 4 * SLOTS]
    refs = refs[4 * SLOTS :]
    outs, beac_out = refs[:TP], refs[TP]
    qs, gs, os, dqs, keys, vals, keys_t, vals_t, bias, scores, probs, dscores, dk_acc, dv_acc = refs[TP + 1 :]
    head = pl.program_id(0)
    me = sc[S_Y]

    @pl.when(head == 0)
    def _():
        same = sc[S_SAME]
        for t, dst in ((0, keys), (1, vals)):
            for j in range(SLOTS):
                a, b = near[t * SLOTS + j][0], far[t * SLOTS + j][0]
                dst[pl.ds(j * BLOCK, BLOCK), :] = jnp.where(same == 1, a, b)
            for d in range(TP):
                at = pl.multiple_of(BEAC + lax.rem(me + d, TP) * CHUNK, CHUNK)
                dst[pl.ds(at, CHUNK), :] = pieces[d][2 + t][...]
        for j in range(SLOTS):
            row = jnp.where(j < sc[S_COUNT], 0.0, NEG)
            bias[pl.ds(j * BLOCK, BLOCK), :] = jnp.full((BLOCK, HD), row, F32)
        keys_t[...] = keys[...].T
        vals_t[...] = vals[...].T
        dk_acc[...] = jnp.zeros_like(dk_acc)
        dv_acc[...] = jnp.zeros_like(dv_acc)

    for d in range(TP):
        at = lax.rem(me + d, TP)
        qs[at] = pieces[d][0][...]
        gs[at] = pieces[d][1][...]
    tables = (keys, vals, keys_t, vals_t, bias, scores, probs, dscores)
    interleave([chunk_steps(i, qs, gs, os, dqs, *tables) for i in range(TP)], 0.3)
    q_all = qs[...].reshape(TP * CHUNK, HD)
    go_all = gs[...].reshape(TP * CHUNK, HD)
    for b in range(KEYS // CHUNK):
        rows = pl.ds(b * CHUNK, CHUNK)
        first = max(0, b - BEAC // CHUNK) * CHUNK
        dv_acc[rows, :] += mm(probs[rows, first:], go_all[first:], NN)
        dk_acc[rows, :] += mm(dscores[rows, first:], q_all[first:], NN)
    at_o = pl.multiple_of(head * HD, HD)
    at_q = pl.multiple_of(QW + head * HD, HD)
    for d in range(TP):
        at = lax.rem(me + d, TP)
        outs[d][:, pl.ds(at_o, HD)] = os[at]
        outs[d][:, pl.ds(at_q, HD)] = dqs[at]

    @pl.when(head == GROUP - 1)
    def _():
        for d in range(TP):
            at = pl.multiple_of(BEAC + lax.rem(me + d, TP) * CHUNK, CHUNK)
            outs[d][:, 2 * QW : 2 * QW + HD] = (dk_acc[pl.ds(at, CHUNK), :] * SCALE).astype(BF16)
            outs[d][:, 2 * QW + HD :] = dv_acc[pl.ds(at, CHUNK), :].astype(BF16)
        for j in range(SLOTS):
            rows = pl.ds(j * BLOCK, BLOCK)
            beac_out[j, :, :HD] = (dk_acc[rows, :] * SCALE).astype(BF16)
            beac_out[j, :, HD:] = dv_acc[rows, :].astype(BF16)


def attn(group, scalars, own, pieces, near, far):
    spec = pl.BlockSpec
    ops, in_specs = [], []
    kv_heads = 2
    for t in range(2):
        ops.append(own[t])
        in_specs.append(
            spec((CHUNK, HD), lambda h, sc: (0, (sc[S_Y] * kv_heads + group) * GROUP + h))
        )
    for t in range(2):
        ops.append(own[2 + t])
        in_specs.append(spec((CHUNK, HD), lambda h, sc: (0, sc[S_Y] * kv_heads + group)))
    for piece in pieces:
        ops += [piece] * 4
        in_specs += [
            spec((CHUNK, HD), lambda h, sc: (0, h)),
            spec((CHUNK, HD), lambda h, sc: (0, GROUP + h)),
            spec((CHUNK, HD), lambda h, sc: (0, 2 * GROUP)),
            spec((CHUNK, HD), lambda h, sc: (0, 2 * GROUP + 1)),
        ]
    for arr, base in ((near, S_A), (far, S_B)):
        for t in range(2):
            for j in range(SLOTS):
                ops.append(arr)
                in_specs.append(
                    spec((1, BLOCK, HD), lambda h, sc, at=base + j, t=t: (sc[at], 0, t))
                )
    out_specs = [spec((CHUNK, PIECE), lambda h, sc: (0, 0)) for _ in range(TP)]
    out_specs.append(spec((SLOTS, BLOCK, 2 * HD), lambda h, sc: (0, 0, 0)))
    out_shape = [jax.ShapeDtypeStruct((CHUNK, PIECE), BF16) for _ in range(TP)]
    out_shape.append(jax.ShapeDtypeStruct((SLOTS, BLOCK, 2 * HD), BF16))
    pairs = GROUP * CHUNK * CHUNK * 18
    return pl.pallas_call(
        attn_body,
        grid_spec=pltpu.PrefetchScalarGridSpec(
            num_scalar_prefetch=1,
            grid=(GROUP,),
            in_specs=in_specs,
            out_specs=out_specs,
            scratch_shapes=[
                pltpu.VMEM((TP, CHUNK, HD), BF16),
                pltpu.VMEM((TP, CHUNK, HD), BF16),
                pltpu.VMEM((TP, CHUNK, HD), BF16),
                pltpu.VMEM((TP, CHUNK, HD), BF16),
                pltpu.VMEM((KEYS, HD), BF16),
                pltpu.VMEM((KEYS, HD), BF16),
                pltpu.VMEM((HD, KEYS), BF16),
                pltpu.VMEM((HD, KEYS), BF16),
                pltpu.VMEM((BEAC, HD), F32),
                pltpu.VMEM((TP, KEYS, CHUNK), F32),
                pltpu.VMEM((KEYS, TP * CHUNK), BF16),
                pltpu.VMEM((KEYS, TP * CHUNK), BF16),
                pltpu.VMEM((KEYS, HD), F32),
                pltpu.VMEM((KEYS, HD), F32),
            ],
        ),
        out_shape=out_shape,
        compiler_params=pltpu.CompilerParams(vmem_limit_bytes=60 << 20),
        cost_estimate=pl.CostEstimate(
            flops=6 * 2 * pairs * HD * 2, bytes_accessed=6 << 20, transcendentals=pairs
        ),
        name="attn",
    )(scalars, *ops)


def split_body(group, y_ref, *refs):
    ins, outs, bufs, in_sems, out_sems = refs[:4], refs[4:7], refs[7], refs[8], refs[9]
    me = y_ref[0]
    loads = []
    for i in range(TP - 1):
        src = lax.rem(me + i + 1, TP) * 2 + group
        row = []
        for t, (at, width) in enumerate(SPANS):
            col = pl.multiple_of(src * width, HD)
            copy = pltpu.make_async_copy(
                ins[t].at[:, pl.ds(col, width)], bufs.at[i, :, pl.ds(at, width)], in_sems.at[i, t]
            )
            copy.start()
            row.append(copy)
        loads.append(row)
    stores = []
    for i in range(TP - 1):
        for copy in loads[i]:
            copy.wait()
        copy = pltpu.make_async_copy(bufs.at[i], outs[i], out_sems.at[i])
        copy.start()
        stores.append(copy)
    for copy in stores:
        copy.wait()


def split(group, y, own):
    anyspec = pl.BlockSpec(memory_space=pl.ANY)
    return pl.pallas_call(
        functools.partial(split_body, group),
        grid_spec=pltpu.PrefetchScalarGridSpec(
            num_scalar_prefetch=1,
            grid=(),
            in_specs=[anyspec] * 4,
            out_specs=[anyspec] * (TP - 1),
            scratch_shapes=[
                pltpu.VMEM((TP - 1, CHUNK, PIECE), BF16),
                pltpu.SemaphoreType.DMA((TP - 1, 4)),
                pltpu.SemaphoreType.DMA((TP - 1,)),
            ],
        ),
        out_shape=[jax.ShapeDtypeStruct((CHUNK, PIECE), BF16)] * (TP - 1),
        compiler_params=pltpu.CompilerParams(vmem_limit_bytes=60 << 20),
        cost_estimate=pl.CostEstimate(flops=0, bytes_accessed=4 << 20, transcendentals=0),
        name="split",
    )(y, *own)


def place_body(group, y_ref, *refs):
    ins, refs = refs[:TP], refs[TP if group == 0 else TP + 4 :]
    outs, bufs, in_sems, out_sems = refs[:4], refs[4], refs[5], refs[6]
    me = y_ref[0]
    loads = [pltpu.make_async_copy(ins[i], bufs.at[i], in_sems.at[i]) for i in range(TP)]
    for copy in loads:
        copy.start()
    stores = []
    for i in range(TP):
        src = lax.rem(me + i, TP) * 2 + group
        loads[i].wait()
        for t, (at, width) in enumerate(SPANS):
            col = pl.multiple_of(src * width, HD)
            copy = pltpu.make_async_copy(
                bufs.at[i, :, pl.ds(at, width)], outs[t].at[:, pl.ds(col, width)], out_sems.at[i, t]
            )
            copy.start()
            stores.append(copy)
    for copy in stores:
        copy.wait()


def place(group, y, pieces, placed):
    anyspec = pl.BlockSpec(memory_space=pl.ANY)
    widths = (TP * 2 * QW, TP * 2 * QW, TP * 2 * HD, TP * 2 * HD)
    return pl.pallas_call(
        functools.partial(place_body, group),
        grid_spec=pltpu.PrefetchScalarGridSpec(
            num_scalar_prefetch=1,
            grid=(),
            in_specs=[anyspec] * (TP + len(placed)),
            out_specs=[anyspec] * 4,
            scratch_shapes=[
                pltpu.VMEM((TP, CHUNK, PIECE), BF16),
                pltpu.SemaphoreType.DMA((TP,)),
                pltpu.SemaphoreType.DMA((TP, 4)),
            ],
        ),
        out_shape=[jax.ShapeDtypeStruct((CHUNK, w), BF16) for w in widths],
        input_output_aliases={1 + TP + t: t for t in range(len(placed))},
        compiler_params=pltpu.CompilerParams(vmem_limit_bytes=60 << 20),
        cost_estimate=pl.CostEstimate(flops=0, bytes_accessed=5 << 20, transcendentals=0),
        name="place",
    )(y, *pieces, *placed)


def table_body(in_ref, out_ref):
    for i in range(in_ref.shape[0]):
        out_ref[i] = in_ref[i]


def through_smem(x):
    smem = pl.BlockSpec(memory_space=pltpu.SMEM)
    return pl.pallas_call(
        table_body,
        in_specs=[smem],
        out_specs=smem,
        out_shape=jax.ShapeDtypeStruct(x.shape, x.dtype),
        name="table",
    )(x)


def shift(x, step):
    return lax.ppermute(x, "y", [(s, (s + step) % TP) for s in range(TP)])


def to_chips(x):
    return lax.all_to_all(x, ("z", "x"), 0, 0, tiled=True)


def swap(x):
    return lax.ppermute(x, "core", [(0, 1), (1, 0)])


def layer(queries, keys_in, values_in, grad_output, beacon_keys, beacon_values, read_blocks, read_counts):
    y = lax.axis_index("y")
    core = lax.axis_index("core")
    chips = lax.axis_size("z") * lax.axis_size("x")

    both = [
        jnp.concatenate(
            [beacon_keys[:, g * HD : (g + 1) * HD], beacon_values[:, g * HD : (g + 1) * HD]], axis=1
        )
        for g in range(2)
    ]
    first = core == 0
    mine = jnp.where(first, both[0], both[1])
    other = swap(jnp.where(first, both[1], both[0]))
    chip_blocks = jnp.broadcast_to(jnp.stack([mine, other])[None], (chips, 2, BLOCK, 2 * HD))
    row, count = read_blocks[0], read_counts
    table = jnp.concatenate([row, count])
    peer_table = swap(table)

    own = (queries, grad_output, keys_in, values_in)
    place_at = y[None].astype(jnp.int32)
    recv = []
    for g in range(2):
        got = {}
        sent = split(g, place_at, own)
        for d in (1, 3, 2):
            got[TP - d] = shift(sent[d - 1], d)
        recv.append([got[1], got[2], got[3]])

    near = to_chips(chip_blocks)
    far = swap(near).reshape(chips * 2, BLOCK, 2 * HD)
    near = near.reshape(chips * 2, BLOCK, 2 * HD)

    chip, parity = row // 2, row % 2
    back, beacs = [], []
    for g in range(2):
        scalars = jnp.concatenate(
            [
                chip * 2 + (parity ^ core),
                chip * 2 + (parity ^ core ^ 1),
                count,
                y[None],
                (core == g).astype(jnp.int32)[None],
            ]
        ).astype(jnp.int32)
        if g == 0:
            scalars = through_smem(scalars)
        res = attn(g, scalars, own, recv[g], near, far)
        got = {0: res[0]}
        for d in (1, 3, 2):
            got[TP - d] = shift(res[d], d)
        back.append([got[d] for d in range(TP)])
        dense = jnp.zeros((chips, BLOCK, 2 * HD), F32)
        ids = jnp.arange(chips, dtype=jnp.int32)
        for terms, tab in ((res[TP], table), (swap(res[TP]), peer_table)):
            for j in range(SLOTS):
                use = ((tab[j] == ids * 2 + core) & (j < tab[SLOTS])).astype(F32)
                dense = dense + use[:, None, None] * terms[j].astype(F32)[None]
        parts = to_chips(dense.astype(BF16))
        beacs.append(jnp.sum(parts.astype(F32), axis=0).astype(BF16))
    placed = ()
    for g in range(2):
        placed = place(g, place_at, back[g], placed)
    out, dq, dk, dv = placed
    dbk = jnp.concatenate([b[:, :HD] for b in beacs], axis=1)
    dbv = jnp.concatenate([b[:, HD:] for b in beacs], axis=1)
    return out, dq, dk, dv, dbk, dbv


def solution(mesh):
    split = Mesh(mesh.devices.reshape(4, 4, 2, 4), ("z", "x", "core", "y"))
    ctx = ("z", "x", "core")
    tokens = P(ctx + ("y",), None)
    beacon = P(ctx, "y")
    in_specs = (tokens,) * 4 + (beacon,) * 2 + (P(ctx, None), P(ctx))
    out_specs = (tokens,) * 4 + (beacon,) * 2
    return jax.shard_map(layer, mesh=split, in_specs=in_specs, out_specs=out_specs, check_vma=False)
```

```python
import functools
import math

import jax
import jax.numpy as jnp
from jax import lax
from jax.experimental import pallas as pl
from jax.experimental.pallas import tpu as pltpu
from jax.sharding import Mesh
from jax.sharding import PartitionSpec as P


HD = 128
SCALE = HD**-0.5
SCALE2 = SCALE * math.log2(math.e)
NEG = -1e30
F32 = jnp.float32
BF16 = jnp.bfloat16
NN = (((1,), (0,)), ((), ()))
NT = (((1,), (1,)), ((), ()))
VMEM = 66_500_000
TP = 4
CHUNK = 256
SLOTS = 4
BLOCK = 128
BEAC = SLOTS * BLOCK
KEYS = BEAC + TP * CHUNK
GROUP = 4
STEP = 2
QW = GROUP * HD
PIECE = 2 * QW + 2 * HD
SPANS = ((0, QW), (QW, QW), (2 * QW, HD), (2 * QW + HD, HD))


def mm(a, b, dims):
    return lax.dot_general(a, b, dims, preferred_element_type=F32)


def fold(x, op):
    return op(x.reshape(x.shape[0] // 8, 8, x.shape[1]), axis=0)


def chunk_steps(chunk, q_ref, go_ref, o_ref, dq_ref, scores, probs, dscores, keys, vals, keys_t, vals_t, bias):
    blocks = BEAC // CHUNK + chunk + 1
    depth = blocks * CHUNK
    cols = slice(chunk * CHUNK, (chunk + 1) * CHUNK)
    scores = scores.at[chunk]
    held = {}

    def at(b):
        return pl.ds(b * CHUNK, CHUNK)

    def score(b):
        s = mm(keys[at(b), :], q_ref[chunk], NT)
        if b < BEAC // CHUNK:
            part = bias[at(b), :]
            s = s + jnp.concatenate([part, part], axis=1)
        if b == blocks - 1:
            key_pos = lax.broadcasted_iota(jnp.int32, (CHUNK, CHUNK), 0)
            query_pos = lax.broadcasted_iota(jnp.int32, (CHUNK, CHUNK), 1)
            s = jnp.where(key_pos <= query_pos, s, NEG)
        scores[at(b), :] = s
        top = fold(s, jnp.max)
        held["top"] = top if b == 0 else jnp.maximum(held["top"], top)

    def peak():
        held["shift"] = jnp.max(held["top"], axis=0, keepdims=True) * SCALE2
        held["sum"] = jnp.zeros((8, CHUNK), F32)

    def weigh(b):
        w = jnp.exp2(scores[at(b), :] * SCALE2 - held["shift"])
        held["sum"] = held["sum"] + fold(w, jnp.sum)
        scores[at(b), :] = w

    def invert():
        held["inv"] = 1.0 / jnp.sum(held["sum"], axis=0, keepdims=True)

    def normal(b):
        p = scores[at(b), :] * held["inv"]
        scores[at(b), :] = p
        probs[at(b), cols] = p.astype(BF16)

    def attend():
        out = mm(vals_t[:, :depth], probs[:depth, cols], NN).T.astype(BF16)
        o_ref[chunk] = out
        prod = go_ref[chunk].astype(F32) * out.astype(F32)
        held["delta"] = lax.dot_general(
            jnp.ones((8, HD), F32), prod, NT, precision=lax.Precision.HIGHEST, preferred_element_type=F32
        )[0:1, :]

    def dscore(b):
        dp = mm(vals[at(b), :], go_ref[chunk], NT)
        dscores[at(b), cols] = (scores[at(b), :] * (dp - held["delta"])).astype(BF16)

    def dquery():
        dq_ref[chunk] = (mm(keys_t[:, :depth], dscores[:depth, cols], NN).T * SCALE).astype(BF16)

    each = range(blocks)
    steps = [functools.partial(score, b) for b in each] + [peak]
    steps += [functools.partial(weigh, b) for b in each] + [invert]
    steps += [functools.partial(normal, b) for b in each] + [attend]
    return steps + [functools.partial(dscore, b) for b in each] + [dquery]


def key_steps(q_ref, go_ref, probs, dscores, dk_acc, dv_acc):
    def terms(b):
        rows = pl.ds(b * CHUNK, CHUNK)
        first = max(0, b - BEAC // CHUNK)
        go = go_ref[first:].reshape(-1, HD)
        dv_acc[rows, :] += mm(probs[rows, first * CHUNK :], go, NN)
        q = q_ref[first:].reshape(-1, HD)
        dk_acc[rows, :] += mm(dscores[rows, first * CHUNK :], q, NN)

    return [functools.partial(terms, b) for b in range(KEYS // CHUNK)]


def interleave(heads, lag, tail_lag):
    items, start, n = [], 0.0, 0
    for chunks, tail in heads:
        end = 0.0
        for steps in chunks:
            items += [(start + t, n, step) for t, step in enumerate(steps)]
            end = max(end, start + len(steps))
            start += lag * len(steps)
            n += 1
        items += [(end + tail_lag * t, n, step) for t, step in enumerate(tail)]
        n += 1
    for _, _, step in sorted(items, key=lambda item: item[:2]):
        step()


S_NEAR, S_COUNT, S_Y, S_CORE, S_OWN, S_PEER, S_GROUP = 0, 4, 5, 6, 7, 12, 17


def attn_body(sc, *refs):
    pieces = [refs[4 * d : 4 * d + 4] for d in range(TP)]
    refs = refs[4 * TP :]
    near, far = refs[: 2 * SLOTS], refs[2 * SLOTS : 4 * SLOTS]
    refs = refs[4 * SLOTS :]
    outs, beac_out = refs[:TP], refs[TP]
    qs, gs, os, dqs, keys, vals, keys_t, vals_t, bias, scores, probs, dscores, dk_acc, dv_acc = refs[TP + 1 :]
    head = pl.program_id(0)
    me = sc[S_Y]

    @pl.when(head == 0)
    def _():
        same = sc[S_CORE]
        for t, dst in ((0, keys), (1, vals)):
            for j in range(SLOTS):
                a, b = near[t * SLOTS + j][0], far[t * SLOTS + j][0]
                dst[pl.ds(j * BLOCK, BLOCK), :] = jnp.where(same == sc[S_GROUP], a, b)
            for d in range(TP):
                at = pl.multiple_of(BEAC + lax.rem(me + d, TP) * CHUNK, CHUNK)
                dst[pl.ds(at, CHUNK), :] = pieces[d][2 + t][...]
        for j in range(SLOTS):
            row = jnp.where(j < sc[S_COUNT], 0.0, NEG)
            bias[pl.ds(j * BLOCK, BLOCK), :] = jnp.full((BLOCK, HD), row, F32)
        keys_t[...] = keys[...].T
        vals_t[...] = vals[...].T
        dk_acc[...] = jnp.zeros_like(dk_acc)
        dv_acc[...] = jnp.zeros_like(dv_acc)

    for d in range(TP):
        at = lax.rem(me + d, TP)
        for e in range(STEP):
            cols = slice(e * HD, (e + 1) * HD)
            qs[e, at] = pieces[d][0][:, cols]
            gs[e, at] = pieces[d][1][:, cols]
    tables = (keys, vals, keys_t, vals_t, bias)
    heads = []
    for e in range(STEP):
        mid = (scores.at[e], probs.at[e], dscores.at[e])
        chunks = [chunk_steps(i, qs.at[e], gs.at[e], os.at[e], dqs.at[e], *mid, *tables) for i in range(TP)]
        heads.append((chunks, key_steps(qs.at[e], gs.at[e], *mid[1:], dk_acc, dv_acc)))
    interleave(heads, 0.3, 2.0)
    for d in range(TP):
        at = lax.rem(me + d, TP)
        for e in range(STEP):
            at_o = pl.multiple_of((head * STEP + e) * HD, HD)
            at_q = pl.multiple_of(QW + (head * STEP + e) * HD, HD)
            outs[d][:, pl.ds(at_o, HD)] = os[e, at]
            outs[d][:, pl.ds(at_q, HD)] = dqs[e, at]

    @pl.when(head == GROUP // STEP - 1)
    def _():
        for d in range(TP):
            at = pl.multiple_of(BEAC + lax.rem(me + d, TP) * CHUNK, CHUNK)
            outs[d][:, 2 * QW : 2 * QW + HD] = (dk_acc[pl.ds(at, CHUNK), :] * SCALE).astype(BF16)
            outs[d][:, 2 * QW + HD :] = dv_acc[pl.ds(at, CHUNK), :].astype(BF16)
        for j in range(SLOTS):
            rows = pl.ds(j * BLOCK, BLOCK)
            beac_out[j, :, :HD] = (dk_acc[rows, :] * SCALE).astype(BF16)
            beac_out[j, :, HD:] = dv_acc[rows, :].astype(BF16)


def attn(scalars, own, pieces, near, far):
    spec = pl.BlockSpec
    ops, in_specs = [], []
    kv_heads = 2
    for t in range(2):
        ops.append(own[t])
        in_specs.append(
            spec((CHUNK, STEP * HD), lambda h, sc: (0, (sc[S_Y] * kv_heads + sc[S_GROUP]) * (GROUP // STEP) + h))
        )
    for t in range(2):
        ops.append(own[2 + t])
        in_specs.append(spec((CHUNK, HD), lambda h, sc: (0, sc[S_Y] * kv_heads + sc[S_GROUP])))
    for piece in pieces:
        ops += [piece] * 4
        in_specs += [
            spec((CHUNK, STEP * HD), lambda h, sc: (0, h)),
            spec((CHUNK, STEP * HD), lambda h, sc: (0, GROUP // STEP + h)),
            spec((CHUNK, HD), lambda h, sc: (0, 2 * GROUP)),
            spec((CHUNK, HD), lambda h, sc: (0, 2 * GROUP + 1)),
        ]
    for t in range(2):
        for j in range(SLOTS):
            ops.append(near)
            in_specs.append(spec((1, BLOCK, HD), lambda h, sc, j=j, t=t: (sc[S_NEAR + j], 0, t)))
    for t in range(2):
        for j in range(SLOTS):
            ops.append(far)
            in_specs.append(spec((1, BLOCK, HD), lambda h, sc, j=j, t=t: (j, 0, t)))
    out_specs = [spec((CHUNK, PIECE), lambda h, sc: (0, 0)) for _ in range(TP)]
    out_specs.append(spec((SLOTS, BLOCK, 2 * HD), lambda h, sc: (0, 0, 0)))
    out_shape = [jax.ShapeDtypeStruct((CHUNK, PIECE), BF16) for _ in range(TP)]
    out_shape.append(jax.ShapeDtypeStruct((SLOTS, BLOCK, 2 * HD), BF16))
    pairs = GROUP * CHUNK * CHUNK * 18
    return pl.pallas_call(
        attn_body,
        grid_spec=pltpu.PrefetchScalarGridSpec(
            num_scalar_prefetch=1,
            grid=(GROUP // STEP,),
            in_specs=in_specs,
            out_specs=out_specs,
            scratch_shapes=[
                pltpu.VMEM((STEP, TP, CHUNK, HD), BF16),
                pltpu.VMEM((STEP, TP, CHUNK, HD), BF16),
                pltpu.VMEM((STEP, TP, CHUNK, HD), BF16),
                pltpu.VMEM((STEP, TP, CHUNK, HD), BF16),
                pltpu.VMEM((KEYS, HD), BF16),
                pltpu.VMEM((KEYS, HD), BF16),
                pltpu.VMEM((HD, KEYS), BF16),
                pltpu.VMEM((HD, KEYS), BF16),
                pltpu.VMEM((BEAC, HD), F32),
                pltpu.VMEM((STEP, TP, KEYS, CHUNK), F32),
                pltpu.VMEM((STEP, KEYS, TP * CHUNK), BF16),
                pltpu.VMEM((STEP, KEYS, TP * CHUNK), BF16),
                pltpu.VMEM((KEYS, HD), F32),
                pltpu.VMEM((KEYS, HD), F32),
            ],
        ),
        out_shape=out_shape,
        compiler_params=pltpu.CompilerParams(vmem_limit_bytes=VMEM),
        cost_estimate=pl.CostEstimate(
            flops=6 * 2 * pairs * HD * 2, bytes_accessed=6 << 20, transcendentals=pairs
        ),
        name="attn",
    )(scalars, *ops)


def split_body(group, y_ref, *refs):
    ins, outs, bufs, in_sems, out_sems = refs[:4], refs[4:7], refs[7], refs[8], refs[9]
    me = y_ref[0]
    loads = []
    for i in range(TP - 1):
        src = lax.rem(me + i + 1, TP) * 2 + group
        row = []
        for t, (at, width) in enumerate(SPANS):
            col = pl.multiple_of(src * width, HD)
            copy = pltpu.make_async_copy(
                ins[t].at[:, pl.ds(col, width)], bufs.at[i, :, pl.ds(at, width)], in_sems.at[i, t]
            )
            copy.start()
            row.append(copy)
        loads.append(row)
    stores = []
    for i in range(TP - 1):
        for copy in loads[i]:
            copy.wait()
        copy = pltpu.make_async_copy(bufs.at[i], outs[i], out_sems.at[i])
        copy.start()
        stores.append(copy)
    for copy in stores:
        copy.wait()


def split(group, y, own):
    anyspec = pl.BlockSpec(memory_space=pl.ANY)
    return pl.pallas_call(
        functools.partial(split_body, group),
        grid_spec=pltpu.PrefetchScalarGridSpec(
            num_scalar_prefetch=1,
            grid=(),
            in_specs=[anyspec] * 4,
            out_specs=[anyspec] * (TP - 1),
            scratch_shapes=[
                pltpu.VMEM((TP - 1, CHUNK, PIECE), BF16),
                pltpu.SemaphoreType.DMA((TP - 1, 4)),
                pltpu.SemaphoreType.DMA((TP - 1,)),
            ],
        ),
        out_shape=[jax.ShapeDtypeStruct((CHUNK, PIECE), BF16)] * (TP - 1),
        compiler_params=pltpu.CompilerParams(vmem_limit_bytes=VMEM),
        cost_estimate=pl.CostEstimate(flops=0, bytes_accessed=4 << 20, transcendentals=0),
        name="split",
    )(y, *own)


def place_body(group, y_ref, *refs):
    ins, refs = refs[:TP], refs[TP if group == 0 else TP + 4 :]
    outs, bufs, in_sems, out_sems = refs[:4], refs[4], refs[5], refs[6]
    me = y_ref[0]
    loads = [pltpu.make_async_copy(ins[i], bufs.at[i], in_sems.at[i]) for i in range(TP)]
    for copy in loads:
        copy.start()
    stores = []
    for i in range(TP):
        src = lax.rem(me + i, TP) * 2 + group
        loads[i].wait()
        for t, (at, width) in enumerate(SPANS):
            col = pl.multiple_of(src * width, HD)
            copy = pltpu.make_async_copy(
                bufs.at[i, :, pl.ds(at, width)], outs[t].at[:, pl.ds(col, width)], out_sems.at[i, t]
            )
            copy.start()
            stores.append(copy)
    for copy in stores:
        copy.wait()


def place(group, y, pieces, placed):
    anyspec = pl.BlockSpec(memory_space=pl.ANY)
    widths = (TP * 2 * QW, TP * 2 * QW, TP * 2 * HD, TP * 2 * HD)
    return pl.pallas_call(
        functools.partial(place_body, group),
        grid_spec=pltpu.PrefetchScalarGridSpec(
            num_scalar_prefetch=1,
            grid=(),
            in_specs=[anyspec] * (TP + len(placed)),
            out_specs=[anyspec] * 4,
            scratch_shapes=[
                pltpu.VMEM((TP, CHUNK, PIECE), BF16),
                pltpu.SemaphoreType.DMA((TP,)),
                pltpu.SemaphoreType.DMA((TP, 4)),
            ],
        ),
        out_shape=[jax.ShapeDtypeStruct((CHUNK, w), BF16) for w in widths],
        input_output_aliases={1 + TP + t: t for t in range(len(placed))},
        compiler_params=pltpu.CompilerParams(vmem_limit_bytes=VMEM),
        cost_estimate=pl.CostEstimate(flops=0, bytes_accessed=5 << 20, transcendentals=0),
        name="place",
    )(y, *pieces, *placed)


def pick_body(tab_ref, *refs):
    for j in range(SLOTS):
        refs[SLOTS][j] = refs[j][0]


def pick(tables, gathered):
    def block(j):
        def at(i, tab):
            b = tab[S_PEER + j]
            return (b - lax.rem(b, 2) + (lax.rem(b, 2) ^ tab[S_CORE]), 0, 0)

        return pl.BlockSpec((1, BLOCK, 2 * HD), at)

    return pl.pallas_call(
        pick_body,
        grid_spec=pltpu.PrefetchScalarGridSpec(
            num_scalar_prefetch=1,
            grid=(1,),
            in_specs=[block(j) for j in range(SLOTS)],
            out_specs=pl.BlockSpec((SLOTS, BLOCK, 2 * HD), lambda i, tab: (0, 0, 0)),
        ),
        out_shape=jax.ShapeDtypeStruct((SLOTS, BLOCK, 2 * HD), BF16),
        compiler_params=pltpu.CompilerParams(vmem_limit_bytes=VMEM),
        cost_estimate=pl.CostEstimate(flops=0, bytes_accessed=1 << 19, transcendentals=0),
        name="pick",
    )(tables, *([gathered] * SLOTS))


def scatter_body(tab_ref, own_ref, peer_ref, out_ref):
    out_ref[...] = jnp.zeros_like(out_ref)
    for terms, base in ((own_ref, S_OWN), (peer_ref, S_PEER)):
        for j in range(SLOTS):
            block = tab_ref[base + j]

            @pl.when((lax.rem(block, 2) == tab_ref[S_CORE]) & (j < tab_ref[base + SLOTS]))
            def _():
                chip = lax.div(block, 2)
                out_ref[chip] = (out_ref[chip].astype(F32) + terms[j].astype(F32)).astype(BF16)


def scatter(tables, own, peer, chips):
    whole = pl.BlockSpec((SLOTS, BLOCK, 2 * HD), lambda i, tab: (0, 0, 0))
    return pl.pallas_call(
        scatter_body,
        grid_spec=pltpu.PrefetchScalarGridSpec(
            num_scalar_prefetch=1,
            grid=(1,),
            in_specs=[whole, whole],
            out_specs=pl.BlockSpec((chips, BLOCK, 2 * HD), lambda i, tab: (0, 0, 0)),
        ),
        out_shape=jax.ShapeDtypeStruct((chips, BLOCK, 2 * HD), BF16),
        compiler_params=pltpu.CompilerParams(vmem_limit_bytes=VMEM),
        cost_estimate=pl.CostEstimate(flops=0, bytes_accessed=2 << 20, transcendentals=0),
        name="scatter",
    )(tables, own, peer)


def total_body(parts_ref, *refs):
    dbk_ref, dbv_ref = refs[-2:]
    total = parts_ref[0].astype(F32)
    for n in range(1, parts_ref.shape[0]):
        total = total + parts_ref[n].astype(F32)
    dbk_ref[...] = total[:, :HD].astype(BF16)
    dbv_ref[...] = total[:, HD:].astype(BF16)


def total(group, parts, summed):
    column = pl.BlockSpec((BLOCK, HD), lambda i: (0, group))
    return pl.pallas_call(
        total_body,
        grid=(1,),
        in_specs=[pl.BlockSpec(parts.shape, lambda i: (0, 0, 0))]
        + [pl.BlockSpec(memory_space=pl.ANY)] * len(summed),
        out_specs=[column] * 2,
        out_shape=[jax.ShapeDtypeStruct((BLOCK, 2 * HD), BF16)] * 2,
        input_output_aliases={1 + t: t for t in range(len(summed))},
        compiler_params=pltpu.CompilerParams(vmem_limit_bytes=VMEM),
        cost_estimate=pl.CostEstimate(flops=0, bytes_accessed=1 << 20, transcendentals=0),
        name="total",
    )(parts, *summed)


def table_body(in_ref, *out_refs):
    for group, out_ref in enumerate(out_refs):
        for i in range(S_GROUP):
            out_ref[i] = in_ref[i]
        out_ref[S_GROUP] = group


def group_tables(x):
    smem = pl.BlockSpec(memory_space=pltpu.SMEM)
    return pl.pallas_call(
        table_body,
        in_specs=[smem],
        out_specs=[smem] * 2,
        out_shape=[jax.ShapeDtypeStruct((S_GROUP + 1,), x.dtype)] * 2,
        name="table",
    )(x)


def shift(x, step):
    return lax.ppermute(x, "y", [(s, (s + step) % TP) for s in range(TP)])


def to_chips(x):
    return lax.all_to_all(x, ("z", "x"), 0, 0, tiled=True)


def swap(x):
    return lax.ppermute(x, "core", [(0, 1), (1, 0)])


def layer(queries, keys_in, values_in, grad_output, beacon_keys, beacon_values, read_blocks, read_counts):
    y = lax.axis_index("y")
    core = lax.axis_index("core")
    chips = lax.axis_size("z") * lax.axis_size("x")

    both = [
        jnp.concatenate(
            [beacon_keys[:, g * HD : (g + 1) * HD], beacon_values[:, g * HD : (g + 1) * HD]], axis=1
        )
        for g in range(2)
    ]
    first = core == 0
    mine = jnp.where(first, both[0], both[1])
    other = swap(jnp.where(first, both[1], both[0]))
    chip_blocks = jnp.broadcast_to(jnp.stack([mine, other])[None], (chips, 2, BLOCK, 2 * HD))
    row, count = read_blocks[0], read_counts
    table = jnp.concatenate([row, count])
    peer_table = swap(table)

    own = (queries, grad_output, keys_in, values_in)
    place_at = y[None].astype(jnp.int32)
    recv = []
    for g in range(2):
        got = {}
        sent = split(g, place_at, own)
        for d in (1, 3, 2):
            got[TP - d] = shift(sent[d - 1], d)
        recv.append([got[1], got[2], got[3]])

    near = to_chips(chip_blocks)
    near = near.reshape(chips * 2, BLOCK, 2 * HD)

    chip, parity = row // 2, row % 2
    scalars = [chip * 2 + (parity ^ core), count, y[None], core[None], table, peer_table]
    scalars = group_tables(jnp.concatenate(scalars).astype(jnp.int32))
    far = swap(pick(scalars[0], near))
    back, summed = [], ()
    for g in range(2):
        res = attn(scalars[g], own, recv[g], near, far)
        got = {0: res[0]}
        for d in (1, 3, 2):
            got[TP - d] = shift(res[d], d)
        back.append([got[d] for d in range(TP)])
        peer = swap(res[TP])
        dense = scatter(scalars[g], res[TP], peer, chips)
        parts = to_chips(dense)
        summed = total(g, parts, summed)
    placed = ()
    for g in range(2):
        placed = place(g, place_at, back[g], placed)
    out, dq, dk, dv = placed
    return out, dq, dk, dv, *summed


def solution(mesh):
    split = Mesh(mesh.devices.reshape(4, 4, 2, 4), ("z", "x", "core", "y"))
    ctx = ("z", "x", "core")
    tokens = P(ctx + ("y",), None)
    beacon = P(ctx, "y")
    in_specs = (tokens,) * 4 + (beacon,) * 2 + (P(ctx, None), P(ctx))
    out_specs = (tokens,) * 4 + (beacon,) * 2
    return jax.shard_map(layer, mesh=split, in_specs=in_specs, out_specs=out_specs, check_vma=False)
```

```python
import functools
import math

import jax
import jax.numpy as jnp
from jax import lax
from jax.experimental import pallas as pl
from jax.experimental.pallas import tpu as pltpu
from jax.sharding import Mesh
from jax.sharding import PartitionSpec as P


HD = 128
SCALE = HD**-0.5
SCALE2 = SCALE * math.log2(math.e)
NEG = -1e30
F32 = jnp.float32
BF16 = jnp.bfloat16
NN = (((1,), (0,)), ((), ()))
NT = (((1,), (1,)), ((), ()))
VMEM = 67_000_000
TP = 4
CHUNK = 256
SLOTS = 4
BLOCK = 128
BEAC = SLOTS * BLOCK
KEYS = BEAC + TP * CHUNK
GROUP = 4
STEP = 2
QW = GROUP * HD
PIECE = 2 * QW + 2 * HD
SPANS = ((0, QW), (QW, QW), (2 * QW, HD), (2 * QW + HD, HD))


def mm(a, b, dims):
    return lax.dot_general(a, b, dims, preferred_element_type=F32)


def fold(x, op):
    return op(x.reshape(x.shape[0] // 8, 8, x.shape[1]), axis=0)


def chunk_steps(chunk, q_ref, go_ref, o_ref, dq_ref, scores, probs, dscores, keys, vals, keys_t, vals_t, bias):
    blocks = BEAC // CHUNK + chunk + 1
    depth = blocks * CHUNK
    cols = slice(chunk * CHUNK, (chunk + 1) * CHUNK)
    scores = scores.at[chunk]
    held = {}

    def at(b):
        return pl.ds(b * CHUNK, CHUNK)

    def score(b):
        s = mm(keys[at(b), :], q_ref[chunk], NT)
        if b < BEAC // CHUNK:
            part = bias[at(b), :]
            s = s + jnp.concatenate([part, part], axis=1)
        if b == blocks - 1:
            key_pos = lax.broadcasted_iota(jnp.int32, (CHUNK, CHUNK), 0)
            query_pos = lax.broadcasted_iota(jnp.int32, (CHUNK, CHUNK), 1)
            s = jnp.where(key_pos <= query_pos, s, NEG)
        scores[at(b), :] = s
        top = fold(s, jnp.max)
        held["top"] = top if b == 0 else jnp.maximum(held["top"], top)

    def peak():
        held["shift"] = jnp.max(held["top"], axis=0, keepdims=True) * SCALE2
        held["sum"] = jnp.zeros((8, CHUNK), F32)

    def weigh(b):
        w = jnp.exp2(scores[at(b), :] * SCALE2 - held["shift"])
        held["sum"] = held["sum"] + fold(w, jnp.sum)
        scores[at(b), :] = w

    def invert():
        held["inv"] = 1.0 / jnp.sum(held["sum"], axis=0, keepdims=True)

    def normal(b):
        p = scores[at(b), :] * held["inv"]
        scores[at(b), :] = p
        probs[at(b), cols] = p.astype(BF16)

    def attend():
        out = mm(vals_t[:, :depth], probs[:depth, cols], NN).T.astype(BF16)
        o_ref[chunk] = out
        prod = go_ref[chunk].astype(F32) * out.astype(F32)
        held["delta"] = lax.dot_general(
            jnp.ones((8, HD), F32), prod, NT, precision=lax.Precision.HIGHEST, preferred_element_type=F32
        )[0:1, :]

    def dscore(b):
        dp = mm(vals[at(b), :], go_ref[chunk], NT)
        dscores[at(b), cols] = (scores[at(b), :] * (dp - held["delta"])).astype(BF16)

    def dquery():
        dq_ref[chunk] = (mm(keys_t[:, :depth], dscores[:depth, cols], NN).T * SCALE).astype(BF16)

    each = range(blocks)
    steps = [functools.partial(score, b) for b in each] + [peak]
    steps += [functools.partial(weigh, b) for b in each] + [invert]
    steps += [functools.partial(normal, b) for b in each] + [attend]
    return steps + [functools.partial(dscore, b) for b in each] + [dquery]


def key_steps(q_ref, go_ref, probs, dscores, dk_acc, dv_acc):
    def terms(b):
        rows = pl.ds(b * CHUNK, CHUNK)
        first = max(0, b - BEAC // CHUNK)
        go = go_ref[first:].reshape(-1, HD)
        dv_acc[rows, :] += mm(probs[rows, first * CHUNK :], go, NN)
        q = q_ref[first:].reshape(-1, HD)
        dk_acc[rows, :] += mm(dscores[rows, first * CHUNK :], q, NN)

    return [functools.partial(terms, b) for b in range(KEYS // CHUNK)]


def interleave(heads, lag, tail_lag):
    items, start, n = [], 0.0, 0
    for chunks, tail in heads:
        end = 0.0
        for steps in chunks:
            items += [(start + t, n, step) for t, step in enumerate(steps)]
            end = max(end, start + len(steps))
            start += lag * len(steps)
            n += 1
        items += [(end + tail_lag * t, n, step) for t, step in enumerate(tail)]
        n += 1
    for _, _, step in sorted(items, key=lambda item: item[:2]):
        step()


S_NEAR, S_COUNT, S_Y, S_CORE, S_OWN, S_PEER, S_GROUP = 0, 4, 5, 6, 7, 12, 17


def attn_body(sc, *refs):
    pieces = [refs[4 * d : 4 * d + 4] for d in range(TP)]
    refs = refs[4 * TP :]
    near, far = refs[: 2 * SLOTS], refs[2 * SLOTS : 4 * SLOTS]
    refs = refs[4 * SLOTS :]
    outs, beac_out = refs[:TP], refs[TP]
    qs, gs, os, dqs, keys, vals, keys_t, vals_t, bias, scores, probs, dscores, dk_acc, dv_acc = refs[TP + 1 :]
    head = pl.program_id(0)
    me = sc[S_Y]

    @pl.when(head == 0)
    def _():
        for t, dst in ((0, keys), (1, vals)):
            for j in range(SLOTS):
                a, b = near[t * SLOTS + j][0], far[t * SLOTS + j][0]
                dst[pl.ds(j * BLOCK, BLOCK), :] = jnp.where(lax.rem(sc[S_OWN + j], 2) == sc[S_CORE], a, b)
            for d in range(TP):
                at = pl.multiple_of(BEAC + lax.rem(me + d, TP) * CHUNK, CHUNK)
                dst[pl.ds(at, CHUNK), :] = pieces[d][2 + t][...]
        for j in range(SLOTS):
            row = jnp.where(j < sc[S_COUNT], 0.0, NEG)
            bias[pl.ds(j * BLOCK, BLOCK), :] = jnp.full((BLOCK, HD), row, F32)
        keys_t[...] = keys[...].T
        vals_t[...] = vals[...].T
        dk_acc[...] = jnp.zeros_like(dk_acc)
        dv_acc[...] = jnp.zeros_like(dv_acc)

    for d in range(TP):
        at = lax.rem(me + d, TP)
        for e in range(STEP):
            cols = slice(e * HD, (e + 1) * HD)
            qs[e, at] = pieces[d][0][:, cols]
            gs[e, at] = pieces[d][1][:, cols]
    tables = (keys, vals, keys_t, vals_t, bias)
    heads = []
    for e in range(STEP):
        mid = (scores.at[e], probs.at[e], dscores.at[e])
        chunks = [chunk_steps(i, qs.at[e], gs.at[e], os.at[e], dqs.at[e], *mid, *tables) for i in range(TP)]
        heads.append((chunks, key_steps(qs.at[e], gs.at[e], *mid[1:], dk_acc, dv_acc)))
    interleave(heads, 0.3, 3.0)
    for d in range(TP):
        at = lax.rem(me + d, TP)
        for e in range(STEP):
            at_o = pl.multiple_of((head * STEP + e) * HD, HD)
            at_q = pl.multiple_of(QW + (head * STEP + e) * HD, HD)
            outs[d][:, pl.ds(at_o, HD)] = os[e, at]
            outs[d][:, pl.ds(at_q, HD)] = dqs[e, at]

    @pl.when(head == GROUP // STEP - 1)
    def _():
        for d in range(TP):
            at = pl.multiple_of(BEAC + lax.rem(me + d, TP) * CHUNK, CHUNK)
            outs[d][:, 2 * QW : 2 * QW + HD] = (dk_acc[pl.ds(at, CHUNK), :] * SCALE).astype(BF16)
            outs[d][:, 2 * QW + HD :] = dv_acc[pl.ds(at, CHUNK), :].astype(BF16)
        for j in range(SLOTS):
            rows = pl.ds(j * BLOCK, BLOCK)
            beac_out[j, :, :HD] = (dk_acc[rows, :] * SCALE).astype(BF16)
            beac_out[j, :, HD:] = dv_acc[rows, :].astype(BF16)


def attn(scalars, own, pieces, near, far):
    spec = pl.BlockSpec
    ops, in_specs = [], []
    kv_heads = 2
    for t in range(2):
        ops.append(own[t])
        in_specs.append(
            spec((CHUNK, STEP * HD), lambda h, sc: (0, (sc[S_Y] * kv_heads + sc[S_GROUP]) * (GROUP // STEP) + h))
        )
    for t in range(2):
        ops.append(own[2 + t])
        in_specs.append(spec((CHUNK, HD), lambda h, sc: (0, sc[S_Y] * kv_heads + sc[S_GROUP])))
    for piece in pieces:
        ops += [piece] * 4
        in_specs += [
            spec((CHUNK, STEP * HD), lambda h, sc: (0, h)),
            spec((CHUNK, STEP * HD), lambda h, sc: (0, GROUP // STEP + h)),
            spec((CHUNK, HD), lambda h, sc: (0, 2 * GROUP)),
            spec((CHUNK, HD), lambda h, sc: (0, 2 * GROUP + 1)),
        ]
    for t in range(2):
        for j in range(SLOTS):
            ops.append(near)
            in_specs.append(spec((1, BLOCK, HD), lambda h, sc, j=j, t=t: (sc[S_NEAR + j], 0, 2 * t + sc[S_GROUP])))
    for t in range(2):
        for j in range(SLOTS):
            ops.append(far)
            in_specs.append(spec((1, BLOCK, HD), lambda h, sc, j=j, t=t: (j, 0, 2 * t + sc[S_GROUP])))
    out_specs = [spec((CHUNK, PIECE), lambda h, sc: (0, 0)) for _ in range(TP)]
    out_specs.append(spec((SLOTS, BLOCK, 2 * HD), lambda h, sc: (0, 0, 0)))
    out_shape = [jax.ShapeDtypeStruct((CHUNK, PIECE), BF16) for _ in range(TP)]
    out_shape.append(jax.ShapeDtypeStruct((SLOTS, BLOCK, 2 * HD), BF16))
    pairs = GROUP * CHUNK * CHUNK * 18
    return pl.pallas_call(
        attn_body,
        grid_spec=pltpu.PrefetchScalarGridSpec(
            num_scalar_prefetch=1,
            grid=(GROUP // STEP,),
            in_specs=in_specs,
            out_specs=out_specs,
            scratch_shapes=[
                pltpu.VMEM((STEP, TP, CHUNK, HD), BF16),
                pltpu.VMEM((STEP, TP, CHUNK, HD), BF16),
                pltpu.VMEM((STEP, TP, CHUNK, HD), BF16),
                pltpu.VMEM((STEP, TP, CHUNK, HD), BF16),
                pltpu.VMEM((KEYS, HD), BF16),
                pltpu.VMEM((KEYS, HD), BF16),
                pltpu.VMEM((HD, KEYS), BF16),
                pltpu.VMEM((HD, KEYS), BF16),
                pltpu.VMEM((BEAC, HD), F32),
                pltpu.VMEM((STEP, TP, KEYS, CHUNK), F32),
                pltpu.VMEM((STEP, KEYS, TP * CHUNK), BF16),
                pltpu.VMEM((STEP, KEYS, TP * CHUNK), BF16),
                pltpu.VMEM((KEYS, HD), F32),
                pltpu.VMEM((KEYS, HD), F32),
            ],
        ),
        out_shape=out_shape,
        compiler_params=pltpu.CompilerParams(vmem_limit_bytes=VMEM),
        cost_estimate=pl.CostEstimate(
            flops=6 * 2 * pairs * HD * 2, bytes_accessed=6 << 20, transcendentals=pairs
        ),
        name="attn",
    )(scalars, *ops)


def split_body(group, y_ref, *refs):
    ins, outs, bufs, in_sems, out_sems = refs[:4], refs[4:7], refs[7], refs[8], refs[9]
    me = y_ref[0]
    loads = []
    for i in range(TP - 1):
        src = lax.rem(me + i + 1, TP) * 2 + group
        row = []
        for t, (at, width) in enumerate(SPANS):
            col = pl.multiple_of(src * width, HD)
            copy = pltpu.make_async_copy(
                ins[t].at[:, pl.ds(col, width)], bufs.at[i, :, pl.ds(at, width)], in_sems.at[i, t]
            )
            copy.start()
            row.append(copy)
        loads.append(row)
    stores = []
    for i in range(TP - 1):
        for copy in loads[i]:
            copy.wait()
        copy = pltpu.make_async_copy(bufs.at[i], outs[i], out_sems.at[i])
        copy.start()
        stores.append(copy)
    for copy in stores:
        copy.wait()


def split(group, y, own):
    anyspec = pl.BlockSpec(memory_space=pl.ANY)
    return pl.pallas_call(
        functools.partial(split_body, group),
        grid_spec=pltpu.PrefetchScalarGridSpec(
            num_scalar_prefetch=1,
            grid=(),
            in_specs=[anyspec] * 4,
            out_specs=[anyspec] * (TP - 1),
            scratch_shapes=[
                pltpu.VMEM((TP - 1, CHUNK, PIECE), BF16),
                pltpu.SemaphoreType.DMA((TP - 1, 4)),
                pltpu.SemaphoreType.DMA((TP - 1,)),
            ],
        ),
        out_shape=[jax.ShapeDtypeStruct((CHUNK, PIECE), BF16)] * (TP - 1),
        compiler_params=pltpu.CompilerParams(vmem_limit_bytes=VMEM),
        cost_estimate=pl.CostEstimate(flops=0, bytes_accessed=4 << 20, transcendentals=0),
        name="split",
    )(y, *own)


def place_body(entries, held, y_ref, *refs):
    n = len(entries)
    ins, refs = refs[:n], refs[n + held :]
    outs, bufs, in_sems, out_sems = refs[:4], refs[4], refs[5], refs[6]
    me = y_ref[0]
    loads = [pltpu.make_async_copy(ins[i], bufs.at[i], in_sems.at[i]) for i in range(n)]
    for copy in loads:
        copy.start()
    stores = []
    for i, (group, d) in enumerate(entries):
        src = lax.rem(me + d, TP) * 2 + group
        loads[i].wait()
        for t, (at, width) in enumerate(SPANS):
            col = pl.multiple_of(src * width, HD)
            copy = pltpu.make_async_copy(
                bufs.at[i, :, pl.ds(at, width)], outs[t].at[:, pl.ds(col, width)], out_sems.at[i, t]
            )
            copy.start()
            stores.append(copy)
    for copy in stores:
        copy.wait()


def place(entries, y, pieces, placed):
    anyspec = pl.BlockSpec(memory_space=pl.ANY)
    widths = (TP * 2 * QW, TP * 2 * QW, TP * 2 * HD, TP * 2 * HD)
    n = len(entries)
    return pl.pallas_call(
        functools.partial(place_body, entries, len(placed)),
        grid_spec=pltpu.PrefetchScalarGridSpec(
            num_scalar_prefetch=1,
            grid=(),
            in_specs=[anyspec] * (n + len(placed)),
            out_specs=[anyspec] * 4,
            scratch_shapes=[
                pltpu.VMEM((n, CHUNK, PIECE), BF16),
                pltpu.SemaphoreType.DMA((n,)),
                pltpu.SemaphoreType.DMA((n, 4)),
            ],
        ),
        out_shape=[jax.ShapeDtypeStruct((CHUNK, w), BF16) for w in widths],
        input_output_aliases={1 + n + t: t for t in range(len(placed))},
        compiler_params=pltpu.CompilerParams(vmem_limit_bytes=VMEM),
        cost_estimate=pl.CostEstimate(flops=0, bytes_accessed=5 << 20, transcendentals=0),
        name="place",
    )(y, *pieces, *placed)


def pick_body(tab_ref, *refs):
    for j in range(SLOTS):
        refs[SLOTS][j] = refs[j][0]


def pick(tables, gathered):
    def block(j):
        def at(i, tab):
            return (lax.div(tab[S_PEER + j], 2), 0, 0)

        return pl.BlockSpec((1,) + gathered.shape[1:], at)

    return pl.pallas_call(
        pick_body,
        grid_spec=pltpu.PrefetchScalarGridSpec(
            num_scalar_prefetch=1,
            grid=(1,),
            in_specs=[block(j) for j in range(SLOTS)],
            out_specs=pl.BlockSpec((SLOTS,) + gathered.shape[1:], lambda i, tab: (0, 0, 0)),
        ),
        out_shape=jax.ShapeDtypeStruct((SLOTS,) + gathered.shape[1:], BF16),
        compiler_params=pltpu.CompilerParams(vmem_limit_bytes=VMEM),
        cost_estimate=pl.CostEstimate(flops=0, bytes_accessed=1 << 20, transcendentals=0),
        name="pick",
    )(tables, *([gathered] * SLOTS))


def scatter_body(tab_ref, own_ref, peer_ref, out_ref):
    out_ref[...] = jnp.zeros_like(out_ref)
    for terms, base in ((own_ref, S_OWN), (peer_ref, S_PEER)):
        for j in range(SLOTS):
            block = tab_ref[base + j]

            @pl.when((lax.rem(block, 2) == tab_ref[S_CORE]) & (j < tab_ref[base + SLOTS]))
            def _():
                chip = lax.div(block, 2)
                out_ref[chip] = (out_ref[chip].astype(F32) + terms[j].astype(F32)).astype(BF16)


def scatter(tables, own, peer, chips):
    whole = pl.BlockSpec((SLOTS, BLOCK, 2 * HD), lambda i, tab: (0, 0, 0))
    return pl.pallas_call(
        scatter_body,
        grid_spec=pltpu.PrefetchScalarGridSpec(
            num_scalar_prefetch=1,
            grid=(1,),
            in_specs=[whole, whole],
            out_specs=pl.BlockSpec((chips, BLOCK, 2 * HD), lambda i, tab: (0, 0, 0)),
        ),
        out_shape=jax.ShapeDtypeStruct((chips, BLOCK, 2 * HD), BF16),
        compiler_params=pltpu.CompilerParams(vmem_limit_bytes=VMEM),
        cost_estimate=pl.CostEstimate(flops=0, bytes_accessed=2 << 20, transcendentals=0),
        name="scatter",
    )(tables, own, peer)


def total_body(parts_ref, *refs):
    dbk_ref, dbv_ref = refs[-2:]
    total = parts_ref[0].astype(F32)
    for n in range(1, parts_ref.shape[0]):
        total = total + parts_ref[n].astype(F32)
    dbk_ref[...] = total[:, :HD].astype(BF16)
    dbv_ref[...] = total[:, HD:].astype(BF16)


def total(group, parts, summed):
    column = pl.BlockSpec((BLOCK, HD), lambda i: (0, group))
    return pl.pallas_call(
        total_body,
        grid=(1,),
        in_specs=[pl.BlockSpec(parts.shape, lambda i: (0, 0, 0))]
        + [pl.BlockSpec(memory_space=pl.ANY)] * len(summed),
        out_specs=[column] * 2,
        out_shape=[jax.ShapeDtypeStruct((BLOCK, 2 * HD), BF16)] * 2,
        input_output_aliases={1 + t: t for t in range(len(summed))},
        compiler_params=pltpu.CompilerParams(vmem_limit_bytes=VMEM),
        cost_estimate=pl.CostEstimate(flops=0, bytes_accessed=1 << 20, transcendentals=0),
        name="total",
    )(parts, *summed)


def table_body(in_ref, *out_refs):
    for group, out_ref in enumerate(out_refs):
        for i in range(S_GROUP):
            out_ref[i] = in_ref[i]
        out_ref[S_GROUP] = group


def group_tables(x):
    smem = pl.BlockSpec(memory_space=pltpu.SMEM)
    return pl.pallas_call(
        table_body,
        in_specs=[smem],
        out_specs=[smem] * 2,
        out_shape=[jax.ShapeDtypeStruct((S_GROUP + 1,), x.dtype)] * 2,
        name="table",
    )(x)


def shift(x, step):
    return lax.ppermute(x, "y", [(s, (s + step) % TP) for s in range(TP)])


def to_chips(x):
    return lax.all_to_all(x, ("z", "x"), 0, 0, tiled=True)


def swap(x):
    return lax.ppermute(x, "core", [(0, 1), (1, 0)])


def layer(queries, keys_in, values_in, grad_output, beacon_keys, beacon_values, read_blocks, read_counts):
    y = lax.axis_index("y")
    core = lax.axis_index("core")
    chips = lax.axis_size("z") * lax.axis_size("x")

    block = jnp.concatenate([beacon_keys, beacon_values], axis=1)
    chip_blocks = jnp.broadcast_to(block[None], (chips,) + block.shape)
    row, count = read_blocks[0], read_counts
    table = jnp.concatenate([row, count])
    peer_table = swap(table)

    own = (queries, grad_output, keys_in, values_in)
    place_at = y[None].astype(jnp.int32)
    recv = []
    for g in range(2):
        got = {}
        sent = split(g, place_at, own)
        for d in (1, 3, 2):
            got[TP - d] = shift(sent[d - 1], d)
        recv.append([got[1], got[2], got[3]])

    near = to_chips(chip_blocks)
    scalars = [row // 2, count, y[None], core[None], table, peer_table]
    scalars = group_tables(jnp.concatenate(scalars).astype(jnp.int32))
    far = swap(pick(scalars[0], near))
    back, summed = [], ()
    for g in range(2):
        res = attn(scalars[g], own, recv[g], near, far)
        got = {0: res[0]}
        for d in (1, 3, 2):
            got[TP - d] = shift(res[d], d)
        back.append([got[d] for d in range(TP)])
        peer = swap(res[TP])
        dense = scatter(scalars[g], res[TP], peer, chips)
        parts = to_chips(dense)
        summed = total(g, parts, summed)
    placed = ()
    for entries in (((0, 0), (0, 1), (0, 2), (0, 3), (1, 0)), ((1, 1), (1, 3), (1, 2))):
        placed = place(entries, place_at, [back[g][d] for g, d in entries], placed)
    out, dq, dk, dv = placed
    return out, dq, dk, dv, *summed


def solution(mesh):
    split = Mesh(mesh.devices.reshape(4, 4, 2, 4), ("z", "x", "core", "y"))
    ctx = ("z", "x", "core")
    tokens = P(ctx + ("y",), None)
    beacon = P(ctx, "y")
    in_specs = (tokens,) * 4 + (beacon,) * 2 + (P(ctx, None), P(ctx))
    out_specs = (tokens,) * 4 + (beacon,) * 2
    return jax.shard_map(layer, mesh=split, in_specs=in_specs, out_specs=out_specs, check_vma=False)
```

```python
import functools
import math

import jax
import jax.numpy as jnp
from jax import lax
from jax.experimental import pallas as pl
from jax.experimental.pallas import tpu as pltpu
from jax.sharding import Mesh
from jax.sharding import PartitionSpec as P


HD = 128
SCALE = HD**-0.5
SCALE2 = SCALE * math.log2(math.e)
NEG = -1e30
F32 = jnp.float32
BF16 = jnp.bfloat16
NN = (((1,), (0,)), ((), ()))
NT = (((1,), (1,)), ((), ()))
VMEM = 67_000_000
TP = 4
CHUNK = 256
SLOTS = 4
BLOCK = 128
BEAC = SLOTS * BLOCK
KEYS = BEAC + TP * CHUNK
GROUP = 4
STEP = 2
QW = GROUP * HD
PIECE = 2 * QW + 2 * HD
SPANS = ((0, QW), (QW, QW), (2 * QW, HD), (2 * QW + HD, HD))


def mm(a, b, dims):
    return lax.dot_general(a, b, dims, preferred_element_type=F32)


def fold(x, op):
    return op(x.reshape(x.shape[0] // 8, 8, x.shape[1]), axis=0)


def chunk_steps(chunk, q_ref, go_ref, o_ref, dq_ref, scores, probs, dscores, keys, vals, keys_t, vals_t, bias):
    blocks = BEAC // CHUNK + chunk + 1
    depth = blocks * CHUNK
    cols = slice(chunk * CHUNK, (chunk + 1) * CHUNK)
    scores = scores.at[chunk]
    held = {}

    def at(b):
        return pl.ds(b * CHUNK, CHUNK)

    def score(b):
        s = mm(keys[at(b), :], q_ref[chunk], NT)
        if b < BEAC // CHUNK:
            part = bias[at(b), :]
            s = s + jnp.concatenate([part, part], axis=1)
        if b == blocks - 1:
            key_pos = lax.broadcasted_iota(jnp.int32, (CHUNK, CHUNK), 0)
            query_pos = lax.broadcasted_iota(jnp.int32, (CHUNK, CHUNK), 1)
            s = jnp.where(key_pos <= query_pos, s, NEG)
        scores[at(b), :] = s
        top = fold(s, jnp.max)
        held["top"] = top if b == 0 else jnp.maximum(held["top"], top)

    def peak():
        held["shift"] = jnp.max(held["top"], axis=0, keepdims=True) * SCALE2
        held["sum"] = jnp.zeros((8, CHUNK), F32)

    def weigh(b):
        w = jnp.exp2(scores[at(b), :] * SCALE2 - held["shift"])
        held["sum"] = held["sum"] + fold(w, jnp.sum)
        scores[at(b), :] = w

    def invert():
        held["inv"] = 1.0 / jnp.sum(held["sum"], axis=0, keepdims=True)

    def normal(b):
        p = scores[at(b), :] * held["inv"]
        scores[at(b), :] = p
        probs[at(b), cols] = p.astype(BF16)

    def attend():
        out = mm(vals_t[:, :depth], probs[:depth, cols], NN).T.astype(BF16)
        o_ref[chunk] = out
        prod = go_ref[chunk].astype(F32) * out.astype(F32)
        held["delta"] = lax.dot_general(
            jnp.ones((8, HD), F32), prod, NT, precision=lax.Precision.HIGHEST, preferred_element_type=F32
        )[0:1, :]

    def dscore(b):
        dp = mm(vals[at(b), :], go_ref[chunk], NT)
        dscores[at(b), cols] = (scores[at(b), :] * (dp - held["delta"])).astype(BF16)

    def dquery():
        dq_ref[chunk] = (mm(keys_t[:, :depth], dscores[:depth, cols], NN).T * SCALE).astype(BF16)

    each = range(blocks)
    steps = [functools.partial(score, b) for b in each] + [peak]
    steps += [functools.partial(weigh, b) for b in each] + [invert]
    steps += [functools.partial(normal, b) for b in each] + [attend]
    return steps + [functools.partial(dscore, b) for b in each] + [dquery]


def key_steps(q_ref, go_ref, probs, dscores, dk_acc, dv_acc):
    def terms(b):
        rows = pl.ds(b * CHUNK, CHUNK)
        first = max(0, b - BEAC // CHUNK)
        go = go_ref[first:].reshape(-1, HD)
        dv_acc[rows, :] += mm(probs[rows, first * CHUNK :], go, NN)
        q = q_ref[first:].reshape(-1, HD)
        dk_acc[rows, :] += mm(dscores[rows, first * CHUNK :], q, NN)

    return [functools.partial(terms, b) for b in range(KEYS // CHUNK)]


def interleave(heads, lag, tail_lag):
    items, start, n = [], 0.0, 0
    for chunks, tail in heads:
        end = 0.0
        for steps in chunks:
            items += [(start + t, n, step) for t, step in enumerate(steps)]
            end = max(end, start + len(steps))
            start += lag * len(steps)
            n += 1
        items += [(end + tail_lag * t, n, step) for t, step in enumerate(tail)]
        n += 1
    for _, _, step in sorted(items, key=lambda item: item[:2]):
        step()


S_NEAR, S_COUNT, S_Y, S_CORE, S_OWN, S_PEER, S_GROUP = 0, 4, 5, 6, 7, 12, 17


def attn_body(sc, *refs):
    pieces = [refs[4 * d : 4 * d + 4] for d in range(TP)]
    refs = refs[4 * TP :]
    near, far = refs[: 2 * SLOTS], refs[2 * SLOTS : 4 * SLOTS]
    refs = refs[4 * SLOTS :]
    outs, beac_out = refs[:TP], refs[TP]
    qs, gs, os, dqs, keys, vals, keys_t, vals_t, bias, scores, probs, dscores, dk_acc, dv_acc, dkv, sems, kv_sems = refs[TP + 1 :]
    head = pl.program_id(0)
    me = sc[S_Y]

    @pl.when(head == 0)
    def _():
        for t, dst in ((0, keys), (1, vals)):
            for j in range(SLOTS):
                a, b = near[t * SLOTS + j][0], far[t * SLOTS + j][0]
                dst[pl.ds(j * BLOCK, BLOCK), :] = jnp.where(lax.rem(sc[S_OWN + j], 2) == sc[S_CORE], a, b)
            for d in range(TP):
                at = pl.multiple_of(BEAC + lax.rem(me + d, TP) * CHUNK, CHUNK)
                dst[pl.ds(at, CHUNK), :] = pieces[d][2 + t][...]
        for j in range(SLOTS):
            row = jnp.where(j < sc[S_COUNT], 0.0, NEG)
            bias[pl.ds(j * BLOCK, BLOCK), :] = jnp.full((BLOCK, HD), row, F32)
        keys_t[...] = keys[...].T
        vals_t[...] = vals[...].T
        dk_acc[...] = jnp.zeros_like(dk_acc)
        dv_acc[...] = jnp.zeros_like(dv_acc)

    for d in range(TP):
        at = lax.rem(me + d, TP)
        for e in range(STEP):
            cols = slice(e * HD, (e + 1) * HD)
            qs[e, at] = pieces[d][0][:, cols]
            gs[e, at] = pieces[d][1][:, cols]
    tables = (keys, vals, keys_t, vals_t, bias)
    heads = []
    for e in range(STEP):
        mid = (scores.at[e], probs.at[e], dscores.at[e])
        chunks = [chunk_steps(i, qs.at[e], gs.at[e], os.at[head * STEP + e], dqs.at[head * STEP + e], *mid, *tables) for i in range(TP)]
        heads.append((chunks, key_steps(qs.at[e], gs.at[e], *mid[1:], dk_acc, dv_acc)))
    interleave(heads, 0.3, 3.0)

    def leave(h, d, t):
        src = (os, dqs)[t].at[h, lax.rem(me + d, TP)]
        col = pl.multiple_of(t * QW + h * HD, HD)
        return pltpu.make_async_copy(src, outs[d].at[:, pl.ds(col, HD)], sems.at[h, d, t])

    for e in range(STEP):
        for d in range(TP):
            for t in range(2):
                leave(head * STEP + e, d, t).start()

    @pl.when(head == GROUP // STEP - 1)
    def _():
        tails = []
        for d in range(TP):
            at = pl.multiple_of(BEAC + lax.rem(me + d, TP) * CHUNK, CHUNK)
            dkv[d, :, :HD] = (dk_acc[pl.ds(at, CHUNK), :] * SCALE).astype(BF16)
            dkv[d, :, HD:] = dv_acc[pl.ds(at, CHUNK), :].astype(BF16)
            tails.append(pltpu.make_async_copy(dkv.at[d], outs[d].at[:, pl.ds(2 * QW, 2 * HD)], kv_sems.at[d]))
            tails[d].start()
        for j in range(SLOTS):
            rows = pl.ds(j * BLOCK, BLOCK)
            beac_out[j, :, :HD] = (dk_acc[rows, :] * SCALE).astype(BF16)
            beac_out[j, :, HD:] = dv_acc[rows, :].astype(BF16)
        for h in range(GROUP):
            for d in range(TP):
                for t in range(2):
                    leave(h, d, t).wait()
        for copy in tails:
            copy.wait()


def attn(scalars, own, pieces, near, far):
    spec = pl.BlockSpec
    ops, in_specs = [], []
    kv_heads = 2
    for t in range(2):
        ops.append(own[t])
        in_specs.append(
            spec((CHUNK, STEP * HD), lambda h, sc: (0, (sc[S_Y] * kv_heads + sc[S_GROUP]) * (GROUP // STEP) + h))
        )
    for t in range(2):
        ops.append(own[2 + t])
        in_specs.append(spec((CHUNK, HD), lambda h, sc: (0, sc[S_Y] * kv_heads + sc[S_GROUP])))
    for piece in pieces:
        ops += [piece] * 4
        in_specs += [
            spec((CHUNK, STEP * HD), lambda h, sc: (0, h)),
            spec((CHUNK, STEP * HD), lambda h, sc: (0, GROUP // STEP + h)),
            spec((CHUNK, HD), lambda h, sc: (0, 2 * GROUP)),
            spec((CHUNK, HD), lambda h, sc: (0, 2 * GROUP + 1)),
        ]
    for t in range(2):
        for j in range(SLOTS):
            ops.append(near)
            in_specs.append(spec((1, BLOCK, HD), lambda h, sc, j=j, t=t: (sc[S_NEAR + j], 0, 2 * t + sc[S_GROUP])))
    for t in range(2):
        for j in range(SLOTS):
            ops.append(far)
            in_specs.append(spec((1, BLOCK, HD), lambda h, sc, j=j, t=t: (j, 0, 2 * t + sc[S_GROUP])))
    out_specs = [spec(memory_space=pl.ANY) for _ in range(TP)]
    out_specs.append(spec((SLOTS, BLOCK, 2 * HD), lambda h, sc: (0, 0, 0)))
    out_shape = [jax.ShapeDtypeStruct((CHUNK, PIECE), BF16) for _ in range(TP)]
    out_shape.append(jax.ShapeDtypeStruct((SLOTS, BLOCK, 2 * HD), BF16))
    pairs = GROUP * CHUNK * CHUNK * 18
    return pl.pallas_call(
        attn_body,
        grid_spec=pltpu.PrefetchScalarGridSpec(
            num_scalar_prefetch=1,
            grid=(GROUP // STEP,),
            in_specs=in_specs,
            out_specs=out_specs,
            scratch_shapes=[
                pltpu.VMEM((STEP, TP, CHUNK, HD), BF16),
                pltpu.VMEM((STEP, TP, CHUNK, HD), BF16),
                pltpu.VMEM((GROUP, TP, CHUNK, HD), BF16),
                pltpu.VMEM((GROUP, TP, CHUNK, HD), BF16),
                pltpu.VMEM((KEYS, HD), BF16),
                pltpu.VMEM((KEYS, HD), BF16),
                pltpu.VMEM((HD, KEYS), BF16),
                pltpu.VMEM((HD, KEYS), BF16),
                pltpu.VMEM((BEAC, HD), F32),
                pltpu.VMEM((STEP, TP, KEYS, CHUNK), F32),
                pltpu.VMEM((STEP, KEYS, TP * CHUNK), BF16),
                pltpu.VMEM((STEP, KEYS, TP * CHUNK), BF16),
                pltpu.VMEM((KEYS, HD), F32),
                pltpu.VMEM((KEYS, HD), F32),
                pltpu.VMEM((TP, CHUNK, 2 * HD), BF16),
                pltpu.SemaphoreType.DMA((GROUP, TP, 2)),
                pltpu.SemaphoreType.DMA((TP,)),
            ],
        ),
        out_shape=out_shape,
        compiler_params=pltpu.CompilerParams(vmem_limit_bytes=VMEM),
        cost_estimate=pl.CostEstimate(
            flops=6 * 2 * pairs * HD * 2, bytes_accessed=6 << 20, transcendentals=pairs
        ),
        name="attn",
    )(scalars, *ops)


def split_body(group, y_ref, *refs):
    ins, outs, bufs, in_sems, out_sems = refs[:4], refs[4:7], refs[7], refs[8], refs[9]
    me = y_ref[0]
    loads = []
    for i in range(TP - 1):
        src = lax.rem(me + i + 1, TP) * 2 + group
        row = []
        for t, (at, width) in enumerate(SPANS):
            col = pl.multiple_of(src * width, HD)
            copy = pltpu.make_async_copy(
                ins[t].at[:, pl.ds(col, width)], bufs.at[i, :, pl.ds(at, width)], in_sems.at[i, t]
            )
            copy.start()
            row.append(copy)
        loads.append(row)
    stores = []
    for i in range(TP - 1):
        for copy in loads[i]:
            copy.wait()
        copy = pltpu.make_async_copy(bufs.at[i], outs[i], out_sems.at[i])
        copy.start()
        stores.append(copy)
    for copy in stores:
        copy.wait()


def split(group, y, own):
    anyspec = pl.BlockSpec(memory_space=pl.ANY)
    return pl.pallas_call(
        functools.partial(split_body, group),
        grid_spec=pltpu.PrefetchScalarGridSpec(
            num_scalar_prefetch=1,
            grid=(),
            in_specs=[anyspec] * 4,
            out_specs=[anyspec] * (TP - 1),
            scratch_shapes=[
                pltpu.VMEM((TP - 1, CHUNK, PIECE), BF16),
                pltpu.SemaphoreType.DMA((TP - 1, 4)),
                pltpu.SemaphoreType.DMA((TP - 1,)),
            ],
        ),
        out_shape=[jax.ShapeDtypeStruct((CHUNK, PIECE), BF16)] * (TP - 1),
        compiler_params=pltpu.CompilerParams(vmem_limit_bytes=VMEM),
        cost_estimate=pl.CostEstimate(flops=0, bytes_accessed=4 << 20, transcendentals=0),
        name="split",
    )(y, *own)


def place_body(entries, held, y_ref, *refs):
    n = len(entries)
    ins, refs = refs[:n], refs[n + held :]
    outs, bufs, in_sems, out_sems = refs[:4], refs[4], refs[5], refs[6]
    me = y_ref[0]
    loads = [pltpu.make_async_copy(ins[i], bufs.at[i], in_sems.at[i]) for i in range(n)]
    for copy in loads:
        copy.start()
    stores = []
    for i, (group, d) in enumerate(entries):
        src = lax.rem(me + d, TP) * 2 + group
        loads[i].wait()
        for t, (at, width) in enumerate(SPANS):
            col = pl.multiple_of(src * width, HD)
            copy = pltpu.make_async_copy(
                bufs.at[i, :, pl.ds(at, width)], outs[t].at[:, pl.ds(col, width)], out_sems.at[i, t]
            )
            copy.start()
            stores.append(copy)
    for copy in stores:
        copy.wait()


def place(entries, y, pieces, placed):
    anyspec = pl.BlockSpec(memory_space=pl.ANY)
    widths = (TP * 2 * QW, TP * 2 * QW, TP * 2 * HD, TP * 2 * HD)
    n = len(entries)
    return pl.pallas_call(
        functools.partial(place_body, entries, len(placed)),
        grid_spec=pltpu.PrefetchScalarGridSpec(
            num_scalar_prefetch=1,
            grid=(),
            in_specs=[anyspec] * (n + len(placed)),
            out_specs=[anyspec] * 4,
            scratch_shapes=[
                pltpu.VMEM((n, CHUNK, PIECE), BF16),
                pltpu.SemaphoreType.DMA((n,)),
                pltpu.SemaphoreType.DMA((n, 4)),
            ],
        ),
        out_shape=[jax.ShapeDtypeStruct((CHUNK, w), BF16) for w in widths],
        input_output_aliases={1 + n + t: t for t in range(len(placed))},
        compiler_params=pltpu.CompilerParams(vmem_limit_bytes=VMEM),
        cost_estimate=pl.CostEstimate(flops=0, bytes_accessed=5 << 20, transcendentals=0),
        name="place",
    )(y, *pieces, *placed)


def spread_body(k_ref, v_ref, out_ref, buf, in_sems, out_sems):
    halves = (buf.at[:, : 2 * HD], buf.at[:, 2 * HD :])
    loads = [pltpu.make_async_copy(r, h, in_sems.at[t]) for t, (r, h) in enumerate(zip((k_ref, v_ref), halves))]
    for copy in loads:
        copy.start()
    for copy in loads:
        copy.wait()
    stores = [pltpu.make_async_copy(buf, out_ref.at[n], out_sems.at[n]) for n in range(out_ref.shape[0])]
    for copy in stores:
        copy.start()
    for copy in stores:
        copy.wait()


def spread(beacon_keys, beacon_values, chips):
    anyspec = pl.BlockSpec(memory_space=pl.ANY)
    return pl.pallas_call(
        spread_body,
        in_specs=[anyspec] * 2,
        out_specs=anyspec,
        out_shape=jax.ShapeDtypeStruct((chips, BLOCK, 4 * HD), BF16),
        scratch_shapes=[
            pltpu.VMEM((BLOCK, 4 * HD), BF16),
            pltpu.SemaphoreType.DMA((2,)),
            pltpu.SemaphoreType.DMA((chips,)),
        ],
        compiler_params=pltpu.CompilerParams(vmem_limit_bytes=VMEM),
        cost_estimate=pl.CostEstimate(flops=0, bytes_accessed=2 << 20, transcendentals=0),
        name="spread",
    )(beacon_keys, beacon_values)


def pick_body(tab_ref, *refs):
    for j in range(SLOTS):
        refs[SLOTS][j] = refs[j][0]


def pick(tables, gathered):
    def block(j):
        def at(i, tab):
            return (lax.div(tab[S_PEER + j], 2), 0, 0)

        return pl.BlockSpec((1,) + gathered.shape[1:], at)

    return pl.pallas_call(
        pick_body,
        grid_spec=pltpu.PrefetchScalarGridSpec(
            num_scalar_prefetch=1,
            grid=(1,),
            in_specs=[block(j) for j in range(SLOTS)],
            out_specs=pl.BlockSpec((SLOTS,) + gathered.shape[1:], lambda i, tab: (0, 0, 0)),
        ),
        out_shape=jax.ShapeDtypeStruct((SLOTS,) + gathered.shape[1:], BF16),
        compiler_params=pltpu.CompilerParams(vmem_limit_bytes=VMEM),
        cost_estimate=pl.CostEstimate(flops=0, bytes_accessed=1 << 20, transcendentals=0),
        name="pick",
    )(tables, *([gathered] * SLOTS))


def scatter_body(tab_ref, own_ref, peer_ref, out_ref):
    out_ref[...] = jnp.zeros_like(out_ref)
    for terms, base in ((own_ref, S_OWN), (peer_ref, S_PEER)):
        for j in range(SLOTS):
            block = tab_ref[base + j]

            @pl.when((lax.rem(block, 2) == tab_ref[S_CORE]) & (j < tab_ref[base + SLOTS]))
            def _():
                chip = lax.div(block, 2)
                out_ref[chip] = (out_ref[chip].astype(F32) + terms[j].astype(F32)).astype(BF16)


def scatter(tables, own, peer, chips):
    whole = pl.BlockSpec((SLOTS, BLOCK, 2 * HD), lambda i, tab: (0, 0, 0))
    return pl.pallas_call(
        scatter_body,
        grid_spec=pltpu.PrefetchScalarGridSpec(
            num_scalar_prefetch=1,
            grid=(1,),
            in_specs=[whole, whole],
            out_specs=pl.BlockSpec((chips, BLOCK, 2 * HD), lambda i, tab: (0, 0, 0)),
        ),
        out_shape=jax.ShapeDtypeStruct((chips, BLOCK, 2 * HD), BF16),
        compiler_params=pltpu.CompilerParams(vmem_limit_bytes=VMEM),
        cost_estimate=pl.CostEstimate(flops=0, bytes_accessed=2 << 20, transcendentals=0),
        name="scatter",
    )(tables, own, peer)


def total_body(parts_ref, *refs):
    dbk_ref, dbv_ref = refs[-2:]
    total = parts_ref[0].astype(F32)
    for n in range(1, parts_ref.shape[0]):
        total = total + parts_ref[n].astype(F32)
    dbk_ref[...] = total[:, :HD].astype(BF16)
    dbv_ref[...] = total[:, HD:].astype(BF16)


def total(group, parts, summed):
    column = pl.BlockSpec((BLOCK, HD), lambda i: (0, group))
    return pl.pallas_call(
        total_body,
        grid=(1,),
        in_specs=[pl.BlockSpec(parts.shape, lambda i: (0, 0, 0))]
        + [pl.BlockSpec(memory_space=pl.ANY)] * len(summed),
        out_specs=[column] * 2,
        out_shape=[jax.ShapeDtypeStruct((BLOCK, 2 * HD), BF16)] * 2,
        input_output_aliases={1 + t: t for t in range(len(summed))},
        compiler_params=pltpu.CompilerParams(vmem_limit_bytes=VMEM),
        cost_estimate=pl.CostEstimate(flops=0, bytes_accessed=1 << 20, transcendentals=0),
        name="total",
    )(parts, *summed)


def table_body(in_ref, *out_refs):
    for group, out_ref in enumerate(out_refs):
        for i in range(S_GROUP):
            out_ref[i] = in_ref[i]
        out_ref[S_GROUP] = group


def group_tables(x):
    smem = pl.BlockSpec(memory_space=pltpu.SMEM)
    return pl.pallas_call(
        table_body,
        in_specs=[smem],
        out_specs=[smem] * 2,
        out_shape=[jax.ShapeDtypeStruct((S_GROUP + 1,), x.dtype)] * 2,
        name="table",
    )(x)


def shift(x, step):
    return lax.ppermute(x, "y", [(s, (s + step) % TP) for s in range(TP)])


def to_chips(x):
    return lax.all_to_all(x, ("z", "x"), 0, 0, tiled=True)


def swap(x):
    return lax.ppermute(x, "core", [(0, 1), (1, 0)])


def layer(queries, keys_in, values_in, grad_output, beacon_keys, beacon_values, read_blocks, read_counts):
    y = lax.axis_index("y")
    core = lax.axis_index("core")
    chips = lax.axis_size("z") * lax.axis_size("x")

    chip_blocks = spread(beacon_keys, beacon_values, chips)
    row, count = read_blocks[0], read_counts
    table = jnp.concatenate([row, count])
    peer_table = swap(table)

    own = (queries, grad_output, keys_in, values_in)
    place_at = y[None].astype(jnp.int32)
    recv = []
    for g in range(2):
        got = {}
        sent = split(g, place_at, own)
        for d in (2, 1, 3):
            got[TP - d] = shift(sent[d - 1], d)
        recv.append([got[1], got[2], got[3]])

    near = to_chips(chip_blocks)
    scalars = [row // 2, count, y[None], core[None], table, peer_table]
    scalars = group_tables(jnp.concatenate(scalars).astype(jnp.int32))
    far = swap(pick(scalars[0], near))
    back, summed = [], ()
    for g in range(2):
        res = attn(scalars[g], own, recv[g], near, far)
        got = {0: res[0]}
        for d in (2, 1, 3):
            got[TP - d] = shift(res[d], d)
        back.append([got[d] for d in range(TP)])
        peer = swap(res[TP])
        dense = scatter(scalars[g], res[TP], peer, chips)
        parts = to_chips(dense)
        summed = total(g, parts, summed)
    placed = ()
    for entries in (((0, 0), (0, 1), (0, 2), (0, 3), (1, 0)), ((1, 1), (1, 3), (1, 2))):
        placed = place(entries, place_at, [back[g][d] for g, d in entries], placed)
    out, dq, dk, dv = placed
    return out, dq, dk, dv, *summed


def solution(mesh):
    split = Mesh(mesh.devices.reshape(4, 4, 2, 4), ("z", "x", "core", "y"))
    ctx = ("z", "x", "core")
    tokens = P(ctx + ("y",), None)
    beacon = P(ctx, "y")
    in_specs = (tokens,) * 4 + (beacon,) * 2 + (P(ctx, None), P(ctx))
    out_specs = (tokens,) * 4 + (beacon,) * 2
    return jax.shard_map(layer, mesh=split, in_specs=in_specs, out_specs=out_specs, check_vma=False)
```

```python
import functools
import math

import jax
import jax.numpy as jnp
from jax import lax
from jax.experimental import pallas as pl
from jax.experimental.pallas import tpu as pltpu
from jax.sharding import Mesh
from jax.sharding import PartitionSpec as P


HD = 128
SCALE = HD**-0.5
SCALE2 = SCALE * math.log2(math.e)
NEG = -1e30
F32 = jnp.float32
BF16 = jnp.bfloat16
NN = (((1,), (0,)), ((), ()))
NT = (((1,), (1,)), ((), ()))
VMEM = 67_000_000
TP = 4
CHUNK = 256
SLOTS = 4
BLOCK = 128
BEAC = SLOTS * BLOCK
KEYS = BEAC + TP * CHUNK
GROUP = 4
STEP = 2
QW = GROUP * HD
PIECE = 2 * QW + 2 * HD
SPANS = ((0, QW), (QW, QW), (2 * QW, HD), (2 * QW + HD, HD))


def mm(a, b, dims):
    return lax.dot_general(a, b, dims, preferred_element_type=F32)


def fold(x, op):
    return op(x.reshape(x.shape[0] // 8, 8, x.shape[1]), axis=0)


def chunk_steps(chunk, q_ref, go_ref, o_ref, dq_ref, scores, probs, dscores, keys, vals, keys_t, vals_t, bias):
    blocks = BEAC // CHUNK + chunk + 1
    depth = blocks * CHUNK
    cols = slice(chunk * CHUNK, (chunk + 1) * CHUNK)
    scores = scores.at[chunk]
    held = {}

    def at(b):
        return pl.ds(b * CHUNK, CHUNK)

    def score(b):
        s = mm(keys[at(b), :], q_ref[chunk], NT)
        if b < BEAC // CHUNK:
            part = bias[at(b), :]
            s = s + jnp.concatenate([part, part], axis=1)
        if b == blocks - 1:
            key_pos = lax.broadcasted_iota(jnp.int32, (CHUNK, CHUNK), 0)
            query_pos = lax.broadcasted_iota(jnp.int32, (CHUNK, CHUNK), 1)
            s = jnp.where(key_pos <= query_pos, s, NEG)
        scores[at(b), :] = s
        top = fold(s, jnp.max)
        held["top"] = top if b == 0 else jnp.maximum(held["top"], top)

    def peak():
        held["shift"] = jnp.max(held["top"], axis=0, keepdims=True) * SCALE2
        held["sum"] = jnp.zeros((8, CHUNK), F32)

    def weigh(b):
        w = jnp.exp2(scores[at(b), :] * SCALE2 - held["shift"])
        held["sum"] = held["sum"] + fold(w, jnp.sum)
        scores[at(b), :] = w

    def invert():
        held["inv"] = 1.0 / jnp.sum(held["sum"], axis=0, keepdims=True)

    def normal(b):
        p = scores[at(b), :] * held["inv"]
        scores[at(b), :] = p
        probs[at(b), cols] = p.astype(BF16)

    def attend():
        out = mm(vals_t[:, :depth], probs[:depth, cols], NN).T.astype(BF16)
        o_ref[chunk] = out
        prod = go_ref[chunk].astype(F32) * out.astype(F32)
        held["delta"] = lax.dot_general(
            jnp.ones((8, HD), F32), prod, NT, precision=lax.Precision.HIGHEST, preferred_element_type=F32
        )[0:1, :]

    def dscore(b):
        dp = mm(vals[at(b), :], go_ref[chunk], NT)
        dscores[at(b), cols] = (scores[at(b), :] * (dp - held["delta"])).astype(BF16)

    def dquery():
        dq_ref[chunk] = (mm(keys_t[:, :depth], dscores[:depth, cols], NN).T * SCALE).astype(BF16)

    each = range(blocks)
    steps = [functools.partial(score, b) for b in each] + [peak]
    steps += [functools.partial(weigh, b) for b in each] + [invert]
    steps += [functools.partial(normal, b) for b in each] + [attend]
    return steps + [functools.partial(dscore, b) for b in each] + [dquery]


def key_steps(q_ref, go_ref, probs, dscores, dk_acc, dv_acc):
    def terms(b):
        rows = pl.ds(b * CHUNK, CHUNK)
        first = max(0, b - BEAC // CHUNK)
        go = go_ref[first:].reshape(-1, HD)
        dv_acc[rows, :] += mm(probs[rows, first * CHUNK :], go, NN)
        q = q_ref[first:].reshape(-1, HD)
        dk_acc[rows, :] += mm(dscores[rows, first * CHUNK :], q, NN)

    return [functools.partial(terms, b) for b in range(KEYS // CHUNK)]


def interleave(heads, lag, tail_lag):
    items, start, n = [], 0.0, 0
    for chunks, tail in heads:
        end = 0.0
        for steps in chunks:
            items += [(start + t, n, step) for t, step in enumerate(steps)]
            end = max(end, start + len(steps))
            start += lag * len(steps)
            n += 1
        items += [(end + tail_lag * t, n, step) for t, step in enumerate(tail)]
        n += 1
    for _, _, step in sorted(items, key=lambda item: item[:2]):
        step()


S_NEAR, S_COUNT, S_Y, S_CORE, S_OWN, S_PEER, S_GROUP = 0, 4, 5, 6, 7, 12, 17


def attn_body(sc, *refs):
    pieces = [refs[:2]] + [refs[4 + 3 * d : 6 + 3 * d] for d in range(TP - 1)]
    pairs = [refs[6 + 3 * d] for d in range(TP - 1)]
    token_keys = [refs[2]] + [p.at[:, :HD] for p in pairs]
    token_vals = [refs[3]] + [p.at[:, HD:] for p in pairs]
    refs = refs[4 + 3 * (TP - 1) :]
    near, far = refs[:SLOTS], refs[SLOTS : 2 * SLOTS]
    refs = refs[2 * SLOTS :]
    outs, beac_out = refs[:TP], refs[TP]
    qs, gs, os, dqs, keys, vals, keys_t, vals_t, bias, scores, probs, dscores, dk_acc, dv_acc = refs[TP + 1 :]
    head = pl.program_id(0)
    me = sc[S_Y]

    @pl.when(head == 0)
    def _():
        for t, dst, token in ((0, keys, token_keys), (1, vals, token_vals)):
            cols = slice(t * HD, (t + 1) * HD)
            for j in range(SLOTS):
                a, b = near[j][0, :, cols], far[j][0, :, cols]
                dst[pl.ds(j * BLOCK, BLOCK), :] = jnp.where(lax.rem(sc[S_OWN + j], 2) == sc[S_CORE], a, b)
            for d in range(TP):
                at = pl.multiple_of(BEAC + lax.rem(me + d, TP) * CHUNK, CHUNK)
                dst[pl.ds(at, CHUNK), :] = token[d][...]
        for j in range(SLOTS):
            row = jnp.where(j < sc[S_COUNT], 0.0, NEG)
            bias[pl.ds(j * BLOCK, BLOCK), :] = jnp.full((BLOCK, HD), row, F32)
        keys_t[...] = keys[...].T
        vals_t[...] = vals[...].T
        dk_acc[...] = jnp.zeros_like(dk_acc)
        dv_acc[...] = jnp.zeros_like(dv_acc)

    for d in range(TP):
        at = lax.rem(me + d, TP)
        for e in range(STEP):
            cols = slice(e * HD, (e + 1) * HD)
            qs[e, at] = pieces[d][0][:, cols]
            gs[e, at] = pieces[d][1][:, cols]
    tables = (keys, vals, keys_t, vals_t, bias)
    heads = []
    for e in range(STEP):
        mid = (scores.at[e], probs.at[e], dscores.at[e])
        chunks = [chunk_steps(i, qs.at[e], gs.at[e], os.at[e], dqs.at[e], *mid, *tables) for i in range(TP)]
        heads.append((chunks, key_steps(qs.at[e], gs.at[e], *mid[1:], dk_acc, dv_acc)))
    interleave(heads, 0.3, 3.0)
    for d in range(TP):
        at = lax.rem(me + d, TP)
        for e in range(STEP):
            at_o = pl.multiple_of((head * STEP + e) * HD, HD)
            at_q = pl.multiple_of(QW + (head * STEP + e) * HD, HD)
            outs[d][:, pl.ds(at_o, HD)] = os[e, at]
            outs[d][:, pl.ds(at_q, HD)] = dqs[e, at]

    @pl.when(head == GROUP // STEP - 1)
    def _():
        for d in range(TP):
            at = pl.multiple_of(BEAC + lax.rem(me + d, TP) * CHUNK, CHUNK)
            outs[d][:, 2 * QW : 2 * QW + HD] = (dk_acc[pl.ds(at, CHUNK), :] * SCALE).astype(BF16)
            outs[d][:, 2 * QW + HD :] = dv_acc[pl.ds(at, CHUNK), :].astype(BF16)
        for j in range(SLOTS):
            rows = pl.ds(j * BLOCK, BLOCK)
            beac_out[j, :, :HD] = (dk_acc[rows, :] * SCALE).astype(BF16)
            beac_out[j, :, HD:] = dv_acc[rows, :].astype(BF16)


def attn(scalars, own, pieces, near, far):
    spec = pl.BlockSpec
    ops, in_specs = [], []
    kv_heads = 2
    for t in range(2):
        ops.append(own[t])
        in_specs.append(
            spec((CHUNK, STEP * HD), lambda h, sc: (0, (sc[S_Y] * kv_heads + sc[S_GROUP]) * (GROUP // STEP) + h))
        )
    for t in range(2):
        ops.append(own[2 + t])
        in_specs.append(spec((CHUNK, HD), lambda h, sc: (0, sc[S_Y] * kv_heads + sc[S_GROUP])))
    for piece in pieces:
        ops += [piece] * 3
        in_specs += [
            spec((CHUNK, STEP * HD), lambda h, sc: (0, h)),
            spec((CHUNK, STEP * HD), lambda h, sc: (0, GROUP // STEP + h)),
            spec((CHUNK, 2 * HD), lambda h, sc: (0, GROUP)),
        ]
    for j in range(SLOTS):
        ops.append(near)
        in_specs.append(spec((1, BLOCK, 2 * HD), lambda h, sc, j=j: (sc[S_NEAR + j], 0, sc[S_GROUP])))
    for j in range(SLOTS):
        ops.append(far)
        in_specs.append(spec((1, BLOCK, 2 * HD), lambda h, sc, j=j: (j, 0, sc[S_GROUP])))
    out_specs = [spec((CHUNK, PIECE), lambda h, sc: (0, 0)) for _ in range(TP)]
    out_specs.append(spec((SLOTS, BLOCK, 2 * HD), lambda h, sc: (0, 0, 0)))
    out_shape = [jax.ShapeDtypeStruct((CHUNK, PIECE), BF16) for _ in range(TP)]
    out_shape.append(jax.ShapeDtypeStruct((SLOTS, BLOCK, 2 * HD), BF16))
    pairs = GROUP * CHUNK * CHUNK * 18
    return pl.pallas_call(
        attn_body,
        grid_spec=pltpu.PrefetchScalarGridSpec(
            num_scalar_prefetch=1,
            grid=(GROUP // STEP,),
            in_specs=in_specs,
            out_specs=out_specs,
            scratch_shapes=[
                pltpu.VMEM((STEP, TP, CHUNK, HD), BF16),
                pltpu.VMEM((STEP, TP, CHUNK, HD), BF16),
                pltpu.VMEM((STEP, TP, CHUNK, HD), BF16),
                pltpu.VMEM((STEP, TP, CHUNK, HD), BF16),
                pltpu.VMEM((KEYS, HD), BF16),
                pltpu.VMEM((KEYS, HD), BF16),
                pltpu.VMEM((HD, KEYS), BF16),
                pltpu.VMEM((HD, KEYS), BF16),
                pltpu.VMEM((BEAC, HD), F32),
                pltpu.VMEM((STEP, TP, KEYS, CHUNK), F32),
                pltpu.VMEM((STEP, KEYS, TP * CHUNK), BF16),
                pltpu.VMEM((STEP, KEYS, TP * CHUNK), BF16),
                pltpu.VMEM((KEYS, HD), F32),
                pltpu.VMEM((KEYS, HD), F32),
            ],
        ),
        out_shape=out_shape,
        compiler_params=pltpu.CompilerParams(vmem_limit_bytes=VMEM),
        cost_estimate=pl.CostEstimate(
            flops=6 * 2 * pairs * HD * 2, bytes_accessed=6 << 20, transcendentals=pairs
        ),
        name="attn",
    )(scalars, *ops)


def split_body(group, y_ref, *refs):
    ins, outs, bufs, in_sems, out_sems = refs[:4], refs[4:7], refs[7], refs[8], refs[9]
    me = y_ref[0]
    loads = []
    for i in range(TP - 1):
        src = lax.rem(me + i + 1, TP) * 2 + group
        row = []
        for t, (at, width) in enumerate(SPANS):
            col = pl.multiple_of(src * width, HD)
            copy = pltpu.make_async_copy(
                ins[t].at[:, pl.ds(col, width)], bufs.at[i, :, pl.ds(at, width)], in_sems.at[i, t]
            )
            copy.start()
            row.append(copy)
        loads.append(row)
    stores = []
    for i in range(TP - 1):
        for copy in loads[i]:
            copy.wait()
        copy = pltpu.make_async_copy(bufs.at[i], outs[i], out_sems.at[i])
        copy.start()
        stores.append(copy)
    for copy in stores:
        copy.wait()


def split(group, y, own):
    anyspec = pl.BlockSpec(memory_space=pl.ANY)
    return pl.pallas_call(
        functools.partial(split_body, group),
        grid_spec=pltpu.PrefetchScalarGridSpec(
            num_scalar_prefetch=1,
            grid=(),
            in_specs=[anyspec] * 4,
            out_specs=[anyspec] * (TP - 1),
            scratch_shapes=[
                pltpu.VMEM((TP - 1, CHUNK, PIECE), BF16),
                pltpu.SemaphoreType.DMA((TP - 1, 4)),
                pltpu.SemaphoreType.DMA((TP - 1,)),
            ],
        ),
        out_shape=[jax.ShapeDtypeStruct((CHUNK, PIECE), BF16)] * (TP - 1),
        compiler_params=pltpu.CompilerParams(vmem_limit_bytes=VMEM),
        cost_estimate=pl.CostEstimate(flops=0, bytes_accessed=4 << 20, transcendentals=0),
        name="split",
    )(y, *own)


def place_body(entries, held, y_ref, *refs):
    n = len(entries)
    ins, refs = refs[:n], refs[n + held :]
    outs, bufs, in_sems, out_sems = refs[:4], refs[4], refs[5], refs[6]
    me = y_ref[0]
    loads = [pltpu.make_async_copy(ins[i], bufs.at[i], in_sems.at[i]) for i in range(n)]
    for copy in loads:
        copy.start()
    stores = []
    for i, (group, d) in enumerate(entries):
        src = lax.rem(me + d, TP) * 2 + group
        loads[i].wait()
        for t, (at, width) in enumerate(SPANS):
            col = pl.multiple_of(src * width, HD)
            copy = pltpu.make_async_copy(
                bufs.at[i, :, pl.ds(at, width)], outs[t].at[:, pl.ds(col, width)], out_sems.at[i, t]
            )
            copy.start()
            stores.append(copy)
    for copy in stores:
        copy.wait()


def place(entries, y, pieces, placed):
    anyspec = pl.BlockSpec(memory_space=pl.ANY)
    widths = (TP * 2 * QW, TP * 2 * QW, TP * 2 * HD, TP * 2 * HD)
    n = len(entries)
    return pl.pallas_call(
        functools.partial(place_body, entries, len(placed)),
        grid_spec=pltpu.PrefetchScalarGridSpec(
            num_scalar_prefetch=1,
            grid=(),
            in_specs=[anyspec] * (n + len(placed)),
            out_specs=[anyspec] * 4,
            scratch_shapes=[
                pltpu.VMEM((n, CHUNK, PIECE), BF16),
                pltpu.SemaphoreType.DMA((n,)),
                pltpu.SemaphoreType.DMA((n, 4)),
            ],
        ),
        out_shape=[jax.ShapeDtypeStruct((CHUNK, w), BF16) for w in widths],
        input_output_aliases={1 + n + t: t for t in range(len(placed))},
        compiler_params=pltpu.CompilerParams(vmem_limit_bytes=VMEM),
        cost_estimate=pl.CostEstimate(flops=0, bytes_accessed=5 << 20, transcendentals=0),
        name="place",
    )(y, *pieces, *placed)


def spread_body(k_ref, v_ref, out_ref, buf, in_sems, out_sems):
    loads = []
    for t, ref in enumerate((k_ref, v_ref)):
        for g in range(2):
            dst = buf.at[:, pl.ds((2 * g + t) * HD, HD)]
            loads.append(pltpu.make_async_copy(ref.at[:, pl.ds(g * HD, HD)], dst, in_sems.at[2 * g + t]))
    for copy in loads:
        copy.start()
    for copy in loads:
        copy.wait()
    stores = [pltpu.make_async_copy(buf, out_ref.at[n], out_sems.at[n]) for n in range(out_ref.shape[0])]
    for copy in stores:
        copy.start()
    for copy in stores:
        copy.wait()


def spread(beacon_keys, beacon_values, chips):
    anyspec = pl.BlockSpec(memory_space=pl.ANY)
    return pl.pallas_call(
        spread_body,
        in_specs=[anyspec] * 2,
        out_specs=anyspec,
        out_shape=jax.ShapeDtypeStruct((chips, BLOCK, 4 * HD), BF16),
        scratch_shapes=[
            pltpu.VMEM((BLOCK, 4 * HD), BF16),
            pltpu.SemaphoreType.DMA((4,)),
            pltpu.SemaphoreType.DMA((chips,)),
        ],
        compiler_params=pltpu.CompilerParams(vmem_limit_bytes=VMEM),
        cost_estimate=pl.CostEstimate(flops=0, bytes_accessed=2 << 20, transcendentals=0),
        name="spread",
    )(beacon_keys, beacon_values)


def pick_body(tab_ref, *refs):
    for j in range(SLOTS):
        refs[SLOTS][j] = refs[j][0]


def pick(tables, gathered):
    def block(j):
        def at(i, tab):
            return (lax.div(tab[S_PEER + j], 2), 0, 0)

        return pl.BlockSpec((1,) + gathered.shape[1:], at)

    return pl.pallas_call(
        pick_body,
        grid_spec=pltpu.PrefetchScalarGridSpec(
            num_scalar_prefetch=1,
            grid=(1,),
            in_specs=[block(j) for j in range(SLOTS)],
            out_specs=pl.BlockSpec((SLOTS,) + gathered.shape[1:], lambda i, tab: (0, 0, 0)),
        ),
        out_shape=jax.ShapeDtypeStruct((SLOTS,) + gathered.shape[1:], BF16),
        compiler_params=pltpu.CompilerParams(vmem_limit_bytes=VMEM),
        cost_estimate=pl.CostEstimate(flops=0, bytes_accessed=1 << 20, transcendentals=0),
        name="pick",
    )(tables, *([gathered] * SLOTS))


def scatter_body(tab_ref, own_ref, peer_ref, out_ref):
    out_ref[...] = jnp.zeros_like(out_ref)
    for terms, base in ((own_ref, S_OWN), (peer_ref, S_PEER)):
        for j in range(SLOTS):
            block = tab_ref[base + j]

            @pl.when((lax.rem(block, 2) == tab_ref[S_CORE]) & (j < tab_ref[base + SLOTS]))
            def _():
                chip = lax.div(block, 2)
                out_ref[chip] = (out_ref[chip].astype(F32) + terms[j].astype(F32)).astype(BF16)


def scatter(tables, own, peer, chips):
    whole = pl.BlockSpec((SLOTS, BLOCK, 2 * HD), lambda i, tab: (0, 0, 0))
    return pl.pallas_call(
        scatter_body,
        grid_spec=pltpu.PrefetchScalarGridSpec(
            num_scalar_prefetch=1,
            grid=(1,),
            in_specs=[whole, whole],
            out_specs=pl.BlockSpec((chips, BLOCK, 2 * HD), lambda i, tab: (0, 0, 0)),
        ),
        out_shape=jax.ShapeDtypeStruct((chips, BLOCK, 2 * HD), BF16),
        compiler_params=pltpu.CompilerParams(vmem_limit_bytes=VMEM),
        cost_estimate=pl.CostEstimate(flops=0, bytes_accessed=2 << 20, transcendentals=0),
        name="scatter",
    )(tables, own, peer)


def total_body(parts_ref, *refs):
    dbk_ref, dbv_ref = refs[-2:]
    total = parts_ref[0].astype(F32)
    for n in range(1, parts_ref.shape[0]):
        total = total + parts_ref[n].astype(F32)
    dbk_ref[...] = total[:, :HD].astype(BF16)
    dbv_ref[...] = total[:, HD:].astype(BF16)


def total(group, parts, summed):
    column = pl.BlockSpec((BLOCK, HD), lambda i: (0, group))
    return pl.pallas_call(
        total_body,
        grid=(1,),
        in_specs=[pl.BlockSpec(parts.shape, lambda i: (0, 0, 0))]
        + [pl.BlockSpec(memory_space=pl.ANY)] * len(summed),
        out_specs=[column] * 2,
        out_shape=[jax.ShapeDtypeStruct((BLOCK, 2 * HD), BF16)] * 2,
        input_output_aliases={1 + t: t for t in range(len(summed))},
        compiler_params=pltpu.CompilerParams(vmem_limit_bytes=VMEM),
        cost_estimate=pl.CostEstimate(flops=0, bytes_accessed=1 << 20, transcendentals=0),
        name="total",
    )(parts, *summed)


def table_body(in_ref, *out_refs):
    for group, out_ref in enumerate(out_refs):
        for i in range(S_GROUP):
            out_ref[i] = in_ref[i]
        out_ref[S_GROUP] = group


def group_tables(x):
    smem = pl.BlockSpec(memory_space=pltpu.SMEM)
    return pl.pallas_call(
        table_body,
        in_specs=[smem],
        out_specs=[smem] * 2,
        out_shape=[jax.ShapeDtypeStruct((S_GROUP + 1,), x.dtype)] * 2,
        name="table",
    )(x)


def shift(x, step):
    return lax.ppermute(x, "y", [(s, (s + step) % TP) for s in range(TP)])


def to_chips(x):
    return lax.all_to_all(x, ("z", "x"), 0, 0, tiled=True)


def swap(x):
    return lax.ppermute(x, "core", [(0, 1), (1, 0)])


def layer(queries, keys_in, values_in, grad_output, beacon_keys, beacon_values, read_blocks, read_counts):
    y = lax.axis_index("y")
    core = lax.axis_index("core")
    chips = lax.axis_size("z") * lax.axis_size("x")

    chip_blocks = spread(beacon_keys, beacon_values, chips)
    row, count = read_blocks[0], read_counts
    table = jnp.concatenate([row, count])
    peer_table = swap(table)

    own = (queries, grad_output, keys_in, values_in)
    place_at = y[None].astype(jnp.int32)
    recv = []
    for g in range(2):
        got = {}
        sent = split(g, place_at, own)
        for d in (2, 1, 3):
            got[TP - d] = shift(sent[d - 1], d)
        recv.append([got[1], got[2], got[3]])

    near = to_chips(chip_blocks)
    scalars = [row // 2, count, y[None], core[None], table, peer_table]
    scalars = group_tables(jnp.concatenate(scalars).astype(jnp.int32))
    far = swap(pick(scalars[0], near))
    back, summed = [], ()
    for g in range(2):
        res = attn(scalars[g], own, recv[g], near, far)
        got = {0: res[0]}
        for d in (1, 3, 2):
            got[TP - d] = shift(res[d], d)
        back.append([got[d] for d in range(TP)])
        peer = swap(res[TP])
        dense = scatter(scalars[g], res[TP], peer, chips)
        parts = to_chips(dense)
        summed = total(g, parts, summed)
    placed = ()
    for entries in (((0, 0), (0, 1), (0, 2), (0, 3), (1, 0)), ((1, 1), (1, 3), (1, 2))):
        placed = place(entries, place_at, [back[g][d] for g, d in entries], placed)
    out, dq, dk, dv = placed
    return out, dq, dk, dv, *summed


def solution(mesh):
    split = Mesh(mesh.devices.reshape(4, 4, 2, 4), ("z", "x", "core", "y"))
    ctx = ("z", "x", "core")
    tokens = P(ctx + ("y",), None)
    beacon = P(ctx, "y")
    in_specs = (tokens,) * 4 + (beacon,) * 2 + (P(ctx, None), P(ctx))
    out_specs = (tokens,) * 4 + (beacon,) * 2
    return jax.shard_map(layer, mesh=split, in_specs=in_specs, out_specs=out_specs, check_vma=False)
```

```python
import functools
import math

import jax
import jax.numpy as jnp
from jax import lax
from jax.experimental import pallas as pl
from jax.experimental.pallas import tpu as pltpu
from jax.sharding import Mesh
from jax.sharding import PartitionSpec as P


HD = 128
SCALE = HD**-0.5
SCALE2 = SCALE * math.log2(math.e)
NEG = -1e30
F32 = jnp.float32
BF16 = jnp.bfloat16
NN = (((1,), (0,)), ((), ()))
NT = (((1,), (1,)), ((), ()))
VMEM = 67_000_000
TP = 4
CHUNK = 256
SLOTS = 4
BLOCK = 128
BEAC = SLOTS * BLOCK
KEYS = BEAC + TP * CHUNK
GROUP = 4
STEP = 2
QW = GROUP * HD
PIECE = 2 * QW + 2 * HD
SPANS = ((0, QW), (QW, QW), (2 * QW, HD), (2 * QW + HD, HD))


def mm(a, b, dims):
    return lax.dot_general(a, b, dims, preferred_element_type=F32)


def fold(x, op):
    return op(x.reshape(x.shape[0] // 8, 8, x.shape[1]), axis=0)


def chunk_steps(chunk, q_ref, go_ref, o_ref, dq_ref, scores, probs, dscores, keys, vals, keys_t, vals_t, bias):
    blocks = BEAC // CHUNK + chunk + 1
    depth = blocks * CHUNK
    cols = slice(chunk * CHUNK, (chunk + 1) * CHUNK)
    scores = scores.at[chunk]
    held = {}

    def at(b):
        return pl.ds(b * CHUNK, CHUNK)

    def score(b):
        s = mm(keys[at(b), :], q_ref[chunk], NT)
        if b < BEAC // CHUNK:
            part = bias[at(b), :]
            s = s + jnp.concatenate([part, part], axis=1)
        if b == blocks - 1:
            key_pos = lax.broadcasted_iota(jnp.int32, (CHUNK, CHUNK), 0)
            query_pos = lax.broadcasted_iota(jnp.int32, (CHUNK, CHUNK), 1)
            s = jnp.where(key_pos <= query_pos, s, NEG)
        scores[at(b), :] = s
        top = fold(s, jnp.max)
        held["top"] = top if b == 0 else jnp.maximum(held["top"], top)

    def peak():
        held["shift"] = jnp.max(held["top"], axis=0, keepdims=True) * SCALE2
        held["sum"] = jnp.zeros((8, CHUNK), F32)

    def weigh(b):
        w = jnp.exp2(scores[at(b), :] * SCALE2 - held["shift"])
        held["sum"] = held["sum"] + fold(w, jnp.sum)
        scores[at(b), :] = w

    def invert():
        held["inv"] = 1.0 / jnp.sum(held["sum"], axis=0, keepdims=True)

    def normal(b):
        p = scores[at(b), :] * held["inv"]
        scores[at(b), :] = p
        probs[at(b), cols] = p.astype(BF16)

    def attend():
        out = mm(vals_t[:, :depth], probs[:depth, cols], NN).T.astype(BF16)
        o_ref[chunk] = out
        prod = go_ref[chunk].astype(F32) * out.astype(F32)
        held["delta"] = lax.dot_general(
            jnp.ones((8, HD), F32), prod, NT, precision=lax.Precision.HIGHEST, preferred_element_type=F32
        )[0:1, :]

    def dscore(b):
        dp = mm(vals[at(b), :], go_ref[chunk], NT)
        dscores[at(b), cols] = (scores[at(b), :] * (dp - held["delta"])).astype(BF16)

    def dquery():
        dq_ref[chunk] = (mm(keys_t[:, :depth], dscores[:depth, cols], NN).T * SCALE).astype(BF16)

    each = range(blocks)
    steps = [functools.partial(score, b) for b in each] + [peak]
    steps += [functools.partial(weigh, b) for b in each] + [invert]
    steps += [functools.partial(normal, b) for b in each] + [attend]
    return steps + [functools.partial(dscore, b) for b in each] + [dquery]


def key_steps(q_ref, go_ref, probs, dscores, dk_acc, dv_acc):
    def terms(b):
        rows = pl.ds(b * CHUNK, CHUNK)
        first = max(0, b - BEAC // CHUNK)
        go = go_ref[first:].reshape(-1, HD)
        dv_acc[rows, :] += mm(probs[rows, first * CHUNK :], go, NN)
        q = q_ref[first:].reshape(-1, HD)
        dk_acc[rows, :] += mm(dscores[rows, first * CHUNK :], q, NN)

    return [functools.partial(terms, b) for b in range(KEYS // CHUNK)]


def interleave(heads, lag, tail_lag):
    items, start, n = [], 0.0, 0
    for chunks, tail in heads:
        end = 0.0
        for steps in chunks:
            items += [(start + t, n, step) for t, step in enumerate(steps)]
            end = max(end, start + len(steps))
            start += lag * len(steps)
            n += 1
        items += [(end + tail_lag * t, n, step) for t, step in enumerate(tail)]
        n += 1
    for _, _, step in sorted(items, key=lambda item: item[:2]):
        step()


S_NEAR, S_COUNT, S_Y, S_CORE, S_OWN, S_PEER, S_GROUP = 0, 4, 5, 6, 7, 12, 17


def attn_body(sc, *refs):
    pieces = [refs[:2]] + [refs[4 + 3 * d : 6 + 3 * d] for d in range(TP - 1)]
    pairs = [refs[6 + 3 * d] for d in range(TP - 1)]
    token_keys = [refs[2]] + [p.at[:, :HD] for p in pairs]
    token_vals = [refs[3]] + [p.at[:, HD:] for p in pairs]
    refs = refs[4 + 3 * (TP - 1) :]
    near, far = refs[:SLOTS], refs[SLOTS : 2 * SLOTS]
    refs = refs[2 * SLOTS :]
    outs, beac_out = refs[:TP], refs[TP]
    qs, gs, os, dqs, keys, vals, keys_t, vals_t, bias, scores, probs, dscores, dk_acc, dv_acc = refs[TP + 1 :]
    head = pl.program_id(0)
    me = sc[S_Y]

    @pl.when(head == 0)
    def _():
        for t, dst, token in ((0, keys, token_keys), (1, vals, token_vals)):
            cols = slice(t * HD, (t + 1) * HD)
            for j in range(SLOTS):
                a, b = near[j][0, :, cols], far[j][0, :, cols]
                dst[pl.ds(j * BLOCK, BLOCK), :] = jnp.where(lax.rem(sc[S_OWN + j], 2) == sc[S_CORE], a, b)
            for d in range(TP):
                at = pl.multiple_of(BEAC + lax.rem(me + d, TP) * CHUNK, CHUNK)
                dst[pl.ds(at, CHUNK), :] = token[d][...]
        for j in range(SLOTS):
            row = jnp.where(j < sc[S_COUNT], 0.0, NEG)
            bias[pl.ds(j * BLOCK, BLOCK), :] = jnp.full((BLOCK, HD), row, F32)
        keys_t[...] = keys[...].T
        vals_t[...] = vals[...].T
        dk_acc[...] = jnp.zeros_like(dk_acc)
        dv_acc[...] = jnp.zeros_like(dv_acc)

    for d in range(TP):
        at = lax.rem(me + d, TP)
        for e in range(STEP):
            cols = slice(e * HD, (e + 1) * HD)
            qs[e, at] = pieces[d][0][:, cols]
            gs[e, at] = pieces[d][1][:, cols]
    tables = (keys, vals, keys_t, vals_t, bias)
    heads = []
    for e in range(STEP):
        mid = (scores.at[e], probs.at[e], dscores.at[e])
        chunks = [chunk_steps(i, qs.at[e], gs.at[e], os.at[e], dqs.at[e], *mid, *tables) for i in range(TP)]
        heads.append((chunks, key_steps(qs.at[e], gs.at[e], *mid[1:], dk_acc, dv_acc)))
    interleave(heads, 0.3, 3.0)
    for d in range(TP):
        at = lax.rem(me + d, TP)
        for e in range(STEP):
            at_o = pl.multiple_of((head * STEP + e) * HD, HD)
            at_q = pl.multiple_of(QW + (head * STEP + e) * HD, HD)
            outs[d][:, pl.ds(at_o, HD)] = os[e, at]
            outs[d][:, pl.ds(at_q, HD)] = dqs[e, at]

    @pl.when(head == GROUP // STEP - 1)
    def _():
        for d in range(TP):
            at = pl.multiple_of(BEAC + lax.rem(me + d, TP) * CHUNK, CHUNK)
            outs[d][:, 2 * QW : 2 * QW + HD] = (dk_acc[pl.ds(at, CHUNK), :] * SCALE).astype(BF16)
            outs[d][:, 2 * QW + HD :] = dv_acc[pl.ds(at, CHUNK), :].astype(BF16)
        for j in range(SLOTS):
            rows = pl.ds(j * BLOCK, BLOCK)
            beac_out[j, :, :HD] = (dk_acc[rows, :] * SCALE).astype(BF16)
            beac_out[j, :, HD:] = dv_acc[rows, :].astype(BF16)


def attn(scalars, own, pieces, near, far):
    spec = pl.BlockSpec
    ops, in_specs = [], []
    kv_heads = 2
    for t in range(2):
        ops.append(own[t])
        in_specs.append(
            spec((CHUNK, STEP * HD), lambda h, sc: (0, (sc[S_Y] * kv_heads + sc[S_GROUP]) * (GROUP // STEP) + h))
        )
    for t in range(2):
        ops.append(own[2 + t])
        in_specs.append(spec((CHUNK, HD), lambda h, sc: (0, sc[S_Y] * kv_heads + sc[S_GROUP])))
    for piece in pieces:
        ops += [piece] * 3
        in_specs += [
            spec((CHUNK, STEP * HD), lambda h, sc: (0, h)),
            spec((CHUNK, STEP * HD), lambda h, sc: (0, GROUP // STEP + h)),
            spec((CHUNK, 2 * HD), lambda h, sc: (0, GROUP)),
        ]
    for j in range(SLOTS):
        ops.append(near)
        in_specs.append(spec((1, BLOCK, 2 * HD), lambda h, sc, j=j: (sc[S_NEAR + j], 0, sc[S_GROUP])))
    for j in range(SLOTS):
        ops.append(far)
        in_specs.append(spec((1, BLOCK, 2 * HD), lambda h, sc, j=j: (j, 0, sc[S_GROUP])))
    out_specs = [spec((CHUNK, PIECE), lambda h, sc: (0, 0)) for _ in range(TP)]
    out_specs.append(spec((SLOTS, BLOCK, 2 * HD), lambda h, sc: (0, 0, 0)))
    out_shape = [jax.ShapeDtypeStruct((CHUNK, PIECE), BF16) for _ in range(TP)]
    out_shape.append(jax.ShapeDtypeStruct((SLOTS, BLOCK, 2 * HD), BF16))
    pairs = GROUP * CHUNK * CHUNK * 18
    return pl.pallas_call(
        attn_body,
        grid_spec=pltpu.PrefetchScalarGridSpec(
            num_scalar_prefetch=1,
            grid=(GROUP // STEP,),
            in_specs=in_specs,
            out_specs=out_specs,
            scratch_shapes=[
                pltpu.VMEM((STEP, TP, CHUNK, HD), BF16),
                pltpu.VMEM((STEP, TP, CHUNK, HD), BF16),
                pltpu.VMEM((STEP, TP, CHUNK, HD), BF16),
                pltpu.VMEM((STEP, TP, CHUNK, HD), BF16),
                pltpu.VMEM((KEYS, HD), BF16),
                pltpu.VMEM((KEYS, HD), BF16),
                pltpu.VMEM((HD, KEYS), BF16),
                pltpu.VMEM((HD, KEYS), BF16),
                pltpu.VMEM((BEAC, HD), F32),
                pltpu.VMEM((STEP, TP, KEYS, CHUNK), F32),
                pltpu.VMEM((STEP, KEYS, TP * CHUNK), BF16),
                pltpu.VMEM((STEP, KEYS, TP * CHUNK), BF16),
                pltpu.VMEM((KEYS, HD), F32),
                pltpu.VMEM((KEYS, HD), F32),
            ],
        ),
        out_shape=out_shape,
        compiler_params=pltpu.CompilerParams(vmem_limit_bytes=VMEM),
        cost_estimate=pl.CostEstimate(
            flops=6 * 2 * pairs * HD * 2, bytes_accessed=6 << 20, transcendentals=pairs
        ),
        name="attn",
    )(scalars, *ops)


def split_body(group, y_ref, *refs):
    ins, outs, bufs, in_sems, out_sems = refs[:4], refs[4:7], refs[7], refs[8], refs[9]
    me = y_ref[0]
    loads = []
    for i in range(TP - 1):
        src = lax.rem(me + i + 1, TP) * 2 + group
        row = []
        for t, (at, width) in enumerate(SPANS):
            col = pl.multiple_of(src * width, HD)
            copy = pltpu.make_async_copy(
                ins[t].at[:, pl.ds(col, width)], bufs.at[i, :, pl.ds(at, width)], in_sems.at[i, t]
            )
            copy.start()
            row.append(copy)
        loads.append(row)
    stores = []
    for i in range(TP - 1):
        for copy in loads[i]:
            copy.wait()
        copy = pltpu.make_async_copy(bufs.at[i], outs[i], out_sems.at[i])
        copy.start()
        stores.append(copy)
    for copy in stores:
        copy.wait()


def split(group, y, own):
    anyspec = pl.BlockSpec(memory_space=pl.ANY)
    return pl.pallas_call(
        functools.partial(split_body, group),
        grid_spec=pltpu.PrefetchScalarGridSpec(
            num_scalar_prefetch=1,
            grid=(),
            in_specs=[anyspec] * 4,
            out_specs=[anyspec] * (TP - 1),
            scratch_shapes=[
                pltpu.VMEM((TP - 1, CHUNK, PIECE), BF16),
                pltpu.SemaphoreType.DMA((TP - 1, 4)),
                pltpu.SemaphoreType.DMA((TP - 1,)),
            ],
        ),
        out_shape=[jax.ShapeDtypeStruct((CHUNK, PIECE), BF16)] * (TP - 1),
        compiler_params=pltpu.CompilerParams(vmem_limit_bytes=VMEM),
        cost_estimate=pl.CostEstimate(flops=0, bytes_accessed=4 << 20, transcendentals=0),
        name="split",
    )(y, *own)


def place_body(entries, held, y_ref, *refs):
    n = len(entries)
    ins, refs = refs[:n], refs[n + held :]
    outs, bufs, in_sems, out_sems = refs[:4], refs[4], refs[5], refs[6]
    me = y_ref[0]
    loads = [pltpu.make_async_copy(ins[i], bufs.at[i], in_sems.at[i]) for i in range(n)]
    for copy in loads:
        copy.start()
    stores = []
    for i, (group, d) in enumerate(entries):
        src = lax.rem(me + d, TP) * 2 + group
        loads[i].wait()
        for t, (at, width) in enumerate(SPANS):
            col = pl.multiple_of(src * width, HD)
            copy = pltpu.make_async_copy(
                bufs.at[i, :, pl.ds(at, width)], outs[t].at[:, pl.ds(col, width)], out_sems.at[i, t]
            )
            copy.start()
            stores.append(copy)
    for copy in stores:
        copy.wait()


def place(entries, y, pieces, placed):
    anyspec = pl.BlockSpec(memory_space=pl.ANY)
    widths = (TP * 2 * QW, TP * 2 * QW, TP * 2 * HD, TP * 2 * HD)
    n = len(entries)
    return pl.pallas_call(
        functools.partial(place_body, entries, len(placed)),
        grid_spec=pltpu.PrefetchScalarGridSpec(
            num_scalar_prefetch=1,
            grid=(),
            in_specs=[anyspec] * (n + len(placed)),
            out_specs=[anyspec] * 4,
            scratch_shapes=[
                pltpu.VMEM((n, CHUNK, PIECE), BF16),
                pltpu.SemaphoreType.DMA((n,)),
                pltpu.SemaphoreType.DMA((n, 4)),
            ],
        ),
        out_shape=[jax.ShapeDtypeStruct((CHUNK, w), BF16) for w in widths],
        input_output_aliases={1 + n + t: t for t in range(len(placed))},
        compiler_params=pltpu.CompilerParams(vmem_limit_bytes=VMEM),
        cost_estimate=pl.CostEstimate(flops=0, bytes_accessed=5 << 20, transcendentals=0),
        name="place",
    )(y, *pieces, *placed)


def spread_body(k_ref, v_ref, out_ref, buf, in_sems, out_sems):
    loads = []
    for t, ref in enumerate((k_ref, v_ref)):
        for g in range(2):
            dst = buf.at[:, pl.ds((2 * g + t) * HD, HD)]
            loads.append(pltpu.make_async_copy(ref.at[:, pl.ds(g * HD, HD)], dst, in_sems.at[2 * g + t]))
    for copy in loads:
        copy.start()
    for copy in loads:
        copy.wait()
    stores = [pltpu.make_async_copy(buf, out_ref.at[n], out_sems.at[n]) for n in range(out_ref.shape[0])]
    for copy in stores:
        copy.start()
    for copy in stores:
        copy.wait()


def spread(beacon_keys, beacon_values, chips):
    anyspec = pl.BlockSpec(memory_space=pl.ANY)
    return pl.pallas_call(
        spread_body,
        in_specs=[anyspec] * 2,
        out_specs=anyspec,
        out_shape=jax.ShapeDtypeStruct((chips, BLOCK, 4 * HD), BF16),
        scratch_shapes=[
            pltpu.VMEM((BLOCK, 4 * HD), BF16),
            pltpu.SemaphoreType.DMA((4,)),
            pltpu.SemaphoreType.DMA((chips,)),
        ],
        compiler_params=pltpu.CompilerParams(vmem_limit_bytes=VMEM),
        cost_estimate=pl.CostEstimate(flops=0, bytes_accessed=2 << 20, transcendentals=0),
        name="spread",
    )(beacon_keys, beacon_values)


def pick_body(tab_ref, *refs):
    for j in range(SLOTS):
        refs[SLOTS][j] = refs[j][0]


def pick(tables, gathered):
    def block(j):
        def at(i, tab):
            return (lax.div(tab[S_PEER + j], 2), 0, 0)

        return pl.BlockSpec((1,) + gathered.shape[1:], at)

    return pl.pallas_call(
        pick_body,
        grid_spec=pltpu.PrefetchScalarGridSpec(
            num_scalar_prefetch=1,
            grid=(1,),
            in_specs=[block(j) for j in range(SLOTS)],
            out_specs=pl.BlockSpec((SLOTS,) + gathered.shape[1:], lambda i, tab: (0, 0, 0)),
        ),
        out_shape=jax.ShapeDtypeStruct((SLOTS,) + gathered.shape[1:], BF16),
        compiler_params=pltpu.CompilerParams(vmem_limit_bytes=VMEM),
        cost_estimate=pl.CostEstimate(flops=0, bytes_accessed=1 << 20, transcendentals=0),
        name="pick",
    )(tables, *([gathered] * SLOTS))


def scatter_body(tab_ref, own_ref, peer_ref, out_ref, held, sems):
    loads = [pltpu.make_async_copy(ref, held.at[t], sems.at[t]) for t, ref in enumerate((own_ref, peer_ref))]
    for copy in loads:
        copy.start()
    out_ref[...] = jnp.zeros_like(out_ref)
    for copy in loads:
        copy.wait()
    for terms, base in ((held.at[0], S_OWN), (held.at[1], S_PEER)):
        for j in range(SLOTS):
            block = tab_ref[base + j]

            @pl.when((lax.rem(block, 2) == tab_ref[S_CORE]) & (j < tab_ref[base + SLOTS]))
            def _():
                chip = lax.div(block, 2)
                out_ref[chip] = (out_ref[chip].astype(F32) + terms[j].astype(F32)).astype(BF16)


def scatter(tables, own, peer, chips):
    whole = pl.BlockSpec(memory_space=pl.ANY)
    return pl.pallas_call(
        scatter_body,
        grid_spec=pltpu.PrefetchScalarGridSpec(
            num_scalar_prefetch=1,
            grid=(1,),
            in_specs=[whole, whole],
            out_specs=pl.BlockSpec((chips, BLOCK, 2 * HD), lambda i, tab: (0, 0, 0)),
            scratch_shapes=[pltpu.VMEM((2, SLOTS, BLOCK, 2 * HD), BF16), pltpu.SemaphoreType.DMA((2,))],
        ),
        out_shape=jax.ShapeDtypeStruct((chips, BLOCK, 2 * HD), BF16),
        compiler_params=pltpu.CompilerParams(vmem_limit_bytes=VMEM),
        cost_estimate=pl.CostEstimate(flops=0, bytes_accessed=2 << 20, transcendentals=0),
        name="scatter",
    )(tables, own, peer)


def total_body(parts_ref, *refs):
    dbk_ref, dbv_ref = refs[-2:]
    total = parts_ref[0].astype(F32)
    for n in range(1, parts_ref.shape[0]):
        total = total + parts_ref[n].astype(F32)
    dbk_ref[...] = total[:, :HD].astype(BF16)
    dbv_ref[...] = total[:, HD:].astype(BF16)


def total(group, parts, summed):
    column = pl.BlockSpec((BLOCK, HD), lambda i: (0, group))
    return pl.pallas_call(
        total_body,
        grid=(1,),
        in_specs=[pl.BlockSpec(parts.shape, lambda i: (0, 0, 0))]
        + [pl.BlockSpec(memory_space=pl.ANY)] * len(summed),
        out_specs=[column] * 2,
        out_shape=[jax.ShapeDtypeStruct((BLOCK, 2 * HD), BF16)] * 2,
        input_output_aliases={1 + t: t for t in range(len(summed))},
        compiler_params=pltpu.CompilerParams(vmem_limit_bytes=VMEM),
        cost_estimate=pl.CostEstimate(flops=0, bytes_accessed=1 << 20, transcendentals=0),
        name="total",
    )(parts, *summed)


def table_body(in_ref, *out_refs):
    for group, out_ref in enumerate(out_refs):
        for i in range(S_GROUP):
            out_ref[i] = in_ref[i]
        out_ref[S_GROUP] = group


def group_tables(x):
    smem = pl.BlockSpec(memory_space=pltpu.SMEM)
    return pl.pallas_call(
        table_body,
        in_specs=[smem],
        out_specs=[smem] * 2,
        out_shape=[jax.ShapeDtypeStruct((S_GROUP + 1,), x.dtype)] * 2,
        name="table",
    )(x)


def shift(x, step):
    return lax.ppermute(x, "y", [(s, (s + step) % TP) for s in range(TP)])


def to_chips(x):
    return lax.all_to_all(x, ("z", "x"), 0, 0, tiled=True)


def swap(x):
    return lax.ppermute(x, "core", [(0, 1), (1, 0)])


def layer(queries, keys_in, values_in, grad_output, beacon_keys, beacon_values, read_blocks, read_counts):
    y = lax.axis_index("y")
    core = lax.axis_index("core")
    chips = lax.axis_size("z") * lax.axis_size("x")

    chip_blocks = spread(beacon_keys, beacon_values, chips)
    row, count = read_blocks[0], read_counts
    table = jnp.concatenate([row, count])
    peer_table = swap(table)

    own = (queries, grad_output, keys_in, values_in)
    place_at = y[None].astype(jnp.int32)
    recv = []
    for g in range(2):
        got = {}
        sent = split(g, place_at, own)
        for d in (2, 1, 3):
            got[TP - d] = shift(sent[d - 1], d)
        recv.append([got[1], got[2], got[3]])

    near = to_chips(chip_blocks)
    scalars = [row // 2, count, y[None], core[None], table, peer_table]
    scalars = group_tables(jnp.concatenate(scalars).astype(jnp.int32))
    far = swap(pick(scalars[0], near))
    back, summed = [], ()
    for g in range(2):
        res = attn(scalars[g], own, recv[g], near, far)
        got = {0: res[0]}
        for d in (1, 3, 2):
            got[TP - d] = shift(res[d], d)
        back.append([got[d] for d in range(TP)])
        peer = swap(res[TP])
        dense = scatter(scalars[g], res[TP], peer, chips)
        parts = to_chips(dense)
        summed = total(g, parts, summed)
    placed = ()
    for entries in (((0, 0), (0, 1), (0, 2), (0, 3), (1, 0)), ((1, 1), (1, 3), (1, 2))):
        placed = place(entries, place_at, [back[g][d] for g, d in entries], placed)
    out, dq, dk, dv = placed
    return out, dq, dk, dv, *summed


def solution(mesh):
    split = Mesh(mesh.devices.reshape(4, 4, 2, 4), ("z", "x", "core", "y"))
    ctx = ("z", "x", "core")
    tokens = P(ctx + ("y",), None)
    beacon = P(ctx, "y")
    in_specs = (tokens,) * 4 + (beacon,) * 2 + (P(ctx, None), P(ctx))
    out_specs = (tokens,) * 4 + (beacon,) * 2
    return jax.shard_map(layer, mesh=split, in_specs=in_specs, out_specs=out_specs, check_vma=False)
```
